256 devices in a mesh: region: 64 (over z, y, core), scen: 4 (over x).
Axes of the slice: x: 4, y: 4, z: 8, core: 2. Of those that a mesh axis runs over, the one named last changes fastest.
Arguments:
- inverse_blocks: float32 [2048, 5, 96, 96], P('region')
- block_cols: int32 [2048, 5], P('region'), may hold values from 0 to 31, as said below
- source_current: float32 [196608], P('region'), may hold values from -6 to 6
- node_decay: float32 [196608], P('region'), may hold values from 0.3 to 0.95
- node_gain: float32 [196608], P('region'), may hold values from 0.05 to 0.5
- voltage_init: float32 [256, 196608], P('scen', 'region'), may hold values from -6 to 6
- branch_init: float32 [256, 196608], P('scen', 'region'), may hold values from -3 to 3
- wave_init: float32 [8, 256, 16384], P(None, 'scen', 'region'), may hold values from -6 to 6
- line_node: int32 [16384], P('region'), may hold values from 0 to 3071
- line_delay: int32 [16384], P('region'), may hold values from 1 to 8, as said below
- line_admittance: float32 [16384], P('region'), may hold values from 0.19 to 1, as said below
- conv_region: int32 [24576, 1], P('region'), may hold values from 0 to 63; in each aligned block of 384 rows (0 to 383, 384 to 767, ...) at most 14 rows name the same one
- conv_node: int32 [24576], P('region'), may hold values from 0 to 3071
- conv_power: float32 [24576], P('region'), may hold values from 0.3 to 3
- conv_gains: float32 [2, 24576], P(None, 'region'), may hold values from 0.2 to 0.9
- conv_init: float32 [2, 256, 24576], P(None, 'scen', 'region'), may hold values from -3 to 3
- fault_node: int32 [256], P('scen'), may hold values from 0 to 196607
- fault_kind: int32 [256], P('scen'), may hold values from 0 to 3
Outputs:
- voltage: float32 [256, 196608], P('scen', 'region')
- branch_history: float32 [256, 196608], P('scen', 'region')
- wave_history: float32 [8, 256, 16384], P(None, 'scen', 'region')
- conv_state: float32 [2, 256, 24576], P(None, 'scen', 'region')
- envelope: float32 [196608], P('region')
The draws below stay inside these ranges and needn't reach their ends.
Inputs may be any that keep to these rules, and one draw needn't show every extreme that they name: `block_cols`: entry 0 of row b is b mod 32; the 5 entries of a row are distinct. `line_delay`: entry r * 2 * 128 + l with l < 128 equals entry ((r - 1) mod 64) * 2 * 128 + 128 + l: both ends of a line have one delay. `line_admittance`: entry r * 2 * 128 + l with l < 128 equals entry ((r - 1) mod 64) * 2 * 128 + 128 + l: both ends of a line have one admittance. `conv_region`: among the converters of one region index of the mesh (aligned blocks of 384 rows), at most 14 lie in one region, and some region gets exactly 14.
All inputs are finite; a program needn't handle non-finite values.
Results may differ from the reference program's by a relative error of at most 0.00011.
Values sent between devices are 32-bit elements; how exact they have to be, the bound alone decides.
A program may use at most 128 MiB of HBM per device.

```python
import math
import jax
import jax.numpy as jnp
import numpy as np
from jax import lax

BLK = 96
NB_DEV = 32
KB = 5
LN = 128
DMAX = 8
STEPS = 4
CONV_DEV = 384
KINDS = 4
REGIONS = 64
NODE_DEV = 3072
NODES = 196608
SCEN = 256
LINES = 8192
CONVERTERS = 24576
CAP = 14
N_REGION = 64


def draw_inverse_blocks(key, part):
    block_rows = NODES // BLK
    noise_key, diagonal_key = jax.random.split(key)
    spread = 0.3 * (BLK * KB) ** (-0.5)
    noise_part = jax.random.normal(noise_key, (block_rows, KB, BLK, BLK), jnp.float32)
    diagonal = jax.random.uniform(diagonal_key, (block_rows, 1, 1), jnp.float32, 0.25, 0.35)
    identity = jnp.eye(BLK, dtype=jnp.float32)
    leading = noise_part[:, 0] * spread + diagonal * identity
    return jnp.concatenate([leading[:, None], noise_part[:, 1:] * spread], axis=1)


def draw_block_cols(key, part):
    block_rows = NODES // BLK
    columns = jnp.arange(NB_DEV, dtype=jnp.int32)
    scores = jax.random.randint(key, (block_rows, NB_DEV), 0, 1 << 20, dtype=jnp.int32) * NB_DEV + columns[None, :]
    own_block = jnp.arange(block_rows, dtype=jnp.int32) % NB_DEV
    scores = jnp.where(columns[None, :] == own_block[:, None], -1, scores)
    return jnp.argsort(scores, axis=1, stable=True)[:, :KB].astype(jnp.int32)


def draw_line_delay(key, part):
    region_count = LINES // LN
    delays = jax.random.randint(key, (region_count, LN), 1, DMAX + 1, dtype=jnp.int32)
    delays = delays.at[0, 0].set(DMAX).at[0, 1].set(1)
    return jnp.concatenate([jnp.roll(delays, 1, axis=0), delays], axis=1).reshape(-1).astype(jnp.int32)


def draw_line_admittance(key, part):
    region_count = LINES // LN
    values = jnp.exp(jax.random.uniform(key, (region_count, LN), jnp.float32, math.log(0.2), 0.0))
    return jnp.concatenate([jnp.roll(values, 1, axis=0), values], axis=1).reshape(-1)


def plant(array, key, low, largest):
    extent = array.shape
    index_at = [jax.random.randint(jax.random.fold_in(key, axis), (), 0, extent[axis]) for axis in range(len(extent))]
    array = array.at[tuple(index_at)].set(low)
    longest = extent.index(max(extent))
    index_at[longest] = (index_at[longest] + 1) % extent[longest]
    return array.at[tuple(index_at)].set(largest)


def levels(stream_key, dims, shards, smallest, top_value):
    level = 1.0
    for position, shards_of in shards:
        heights = jax.random.uniform(jax.random.fold_in(jax.random.fold_in(stream_key, 6), position), (shards_of,), jnp.float32, smallest / len(shards), top_value / len(shards))
        level = level * jnp.repeat(jnp.exp(heights), dims[position] // shards_of).reshape((-1,) + (1,) * (len(dims) - 1 - position))
    return level


def routed_block(key, own, number, rows, number_of, top, reach, slope):
    ranking = jax.random.permutation(key, number_of)
    heavy_load, usual = portions_of(number_of, rows * top, reach, slope, True), portions_of(number_of, rows * top, reach, slope, False)
    places = jnp.arange(number_of)

    def named(tallies, rotation):
        used = int((tallies > 0).sum())
        fixed = max(1, used // 4)
        passed = fixed + (places - fixed + rotation * (used - fixed)) % max(1, number_of - fixed)
        return jnp.zeros((number_of,), jnp.int32).at[ranking[jnp.where(places < fixed, places, passed)]].set(jnp.asarray(tallies, jnp.int32))

    tallies = jnp.where(number % 4 == 0, named(heavy_load, number // 4), named(usual, number - number // 4 - 1))
    mixed = jax.random.permutation(jax.random.fold_in(own, 3), number_of)
    source_of, taker = mixed[0:number_of // 2 * 2:2], mixed[1:number_of // 2 * 2:2]
    slack = jnp.minimum(tallies[source_of] - 1, reach - tallies[taker]) // 2
    slack = jnp.where((source_of == ranking[0]) | (taker == ranking[0]) | (tallies[taker] == 0), 0, jnp.maximum(slack, 0))
    passed = jax.random.randint(jax.random.fold_in(own, 4), (number_of // 2,), 0, 1 << 20) % (slack + 1)
    tallies = tallies.at[source_of].add(-passed).at[taker].add(passed)
    members = jnp.searchsorted(jnp.cumsum(tallies), jnp.arange(rows * top), side="right").astype(jnp.int32)
    grid = members.reshape(top, rows).T
    grid = grid[jax.random.permutation(jax.random.fold_in(own, 1), rows)]
    rotation = jax.random.randint(jax.random.fold_in(own, 2), (rows, 1), 0, top)
    return jnp.take_along_axis(grid, (jnp.arange(top)[None, :] + rotation) % top, axis=1)


def portions_of(number_of, total, most, slope, full):
    weights = [(1 << 20) // math.isqrt(grade ** slope) + 1 for grade in range(1, number_of + 1)]
    largest = most if full else min(most, max(-(-total // number_of), total * weights[0] // sum(weights)))
    least = 1 if total - largest >= number_of - 1 else 0
    counts, rest = [largest] + [least] * (number_of - 1), total - largest - least * (number_of - 1)
    while rest > 0:
        candidates = [i for i in range(1, number_of) if counts[i] < largest] or [i for i in range(1, number_of) if counts[i] < most]
        pool, remaining = sum([weights[i] for i in candidates]), rest
        for i in candidates:
            addition = min(most - counts[i], max(1, remaining * weights[i] // pool), rest)
            counts[i] = counts[i] + addition
            rest = rest - addition
    return np.array(counts)


def scatter_about(stream_key, extent, scale, reach, cuts=(), kind=jnp.bfloat16):
    loudness = levels(stream_key, extent, cuts, -0.22, 0.18) if cuts else 1.0
    result = jax.random.normal(stream_key, extent, jnp.float32) * scale * loudness
    return jnp.minimum(jnp.maximum(result, -reach), reach).astype(kind)


def setup_inputs(seed: int = 0) -> dict:
    splits = jax.random.split(jax.random.key(seed), 19)
    inverse_blocks = draw_inverse_blocks(jax.random.fold_in(splits[18], 71), 0)
    block_cols = draw_block_cols(jax.random.fold_in(splits[18], 71), 0)
    source_current = scatter_about(splits[2], (NODES,), 1.0, 6.0, ((0, 64),), jnp.float32)
    node_decay = jnp.clip(0.3 + 0.65 * jax.random.uniform(splits[3], (NODES,), jnp.float32) ** levels(splits[3], (NODES,), ((0, 64),), -0.2, 0.2), 0.3, 0.95)
    node_gain = jnp.clip(jnp.exp(math.log(0.5) - 2.3025851 * jax.random.uniform(splits[4], (NODES,), jnp.float32) ** levels(splits[4], (NODES,), ((0, 64),), -0.2, 0.2)), 0.05, 0.5)
    voltage_init = scatter_about(splits[5], (SCEN, NODES), 1.0, 6.0, ((0, 4), (1, 64)), jnp.float32)
    branch_init = scatter_about(splits[6], (SCEN, NODES), 0.5, 3.0, ((0, 4), (1, 64)), jnp.float32)
    wave_init = scatter_about(splits[7], (DMAX, SCEN, 2 * LINES), 1.0, 6.0, ((1, 4), (2, 64)), jnp.float32)
    line_node = plant(jax.random.randint(splits[8], (2 * LINES,), 0, NODE_DEV), jax.random.fold_in(splits[8], 1), 0, NODE_DEV - 1).astype(jnp.int32)
    line_delay = draw_line_delay(jax.random.fold_in(splits[18], 71), 0)
    line_admittance = draw_line_admittance(jax.random.fold_in(splits[18], 71), 0)
    conv_region_keys = jax.random.split(jax.random.fold_in(splits[11], 1), CONVERTERS // CONV_DEV)
    conv_region_turns = jax.random.permutation(jax.random.fold_in(splits[11], 3), CONVERTERS // CONV_DEV)
    conv_region = jax.vmap(lambda own, number: routed_block(jax.random.fold_in(splits[11], 2), own, number, CONV_DEV, REGIONS, 1, CAP, 1))(conv_region_keys, conv_region_turns).reshape((CONVERTERS, 1))
    conv_node = plant(jax.random.randint(splits[12], (CONVERTERS,), 0, NODE_DEV), jax.random.fold_in(splits[12], 1), 0, NODE_DEV - 1).astype(jnp.int32)
    conv_power = jnp.clip(jnp.exp(math.log(3.0) - 2.3025851 * jax.random.uniform(splits[13], (CONVERTERS,), jnp.float32) ** levels(splits[13], (CONVERTERS,), ((0, 64),), -0.2, 0.2)), 0.3, 3.0)
    conv_gains = jnp.clip(0.2 + 0.7 * jax.random.uniform(splits[14], (2, CONVERTERS), jnp.float32) ** levels(splits[14], (2, CONVERTERS), ((1, 64),), -0.2, 0.2), 0.2, 0.9)
    conv_init = scatter_about(splits[15], (2, SCEN, CONVERTERS), 0.5, 3.0, ((1, 4), (2, 64)), jnp.float32)
    fault_node = plant(jax.random.randint(splits[16], (SCEN,), 0, NODES), jax.random.fold_in(splits[16], 1), 0, NODES - 1).astype(jnp.int32)
    fault_kind = plant(jax.random.randint(splits[17], (SCEN,), 0, KINDS), jax.random.fold_in(splits[17], 1), 0, KINDS - 1).astype(jnp.int32)
    return {"inverse_blocks": inverse_blocks, "block_cols": block_cols, "source_current": source_current, "node_decay": node_decay, "node_gain": node_gain, "voltage_init": voltage_init, "branch_init": branch_init, "wave_init": wave_init, "line_node": line_node, "line_delay": line_delay, "line_admittance": line_admittance, "conv_region": conv_region, "conv_node": conv_node, "conv_power": conv_power, "conv_gains": conv_gains, "conv_init": conv_init, "fault_node": fault_node, "fault_kind": fault_kind}


def apply_inverse(inverse_blocks, global_cols, current):
    scen_count = current.shape[0]
    block_rows = inverse_blocks.shape[0]
    block_width = inverse_blocks.shape[2]
    blocks = current.reshape(scen_count, block_rows, block_width)
    summed = jnp.zeros((scen_count, block_rows, block_width), jnp.float32)
    for column in range(inverse_blocks.shape[1]):
        picked = jnp.take(blocks, global_cols[:, column], axis=1)
        summed = summed + jnp.einsum('sbi,boi->sbo', picked, inverse_blocks[:, column], precision=lax.Precision.HIGHEST)
    return summed.reshape(scen_count, block_rows * block_width)


def reference(inverse_blocks, block_cols, source_current, node_decay, node_gain, voltage_init, branch_init, wave_init, line_node, line_delay, line_admittance, conv_region, conv_node, conv_power, conv_gains, conv_init, fault_node, fault_kind):
    region_count = N_REGION
    block_rows = inverse_blocks.shape[0]
    region_of_block = jnp.arange(block_rows, dtype=jnp.int32) // NB_DEV
    global_cols = (region_of_block[:, None] * NB_DEV + block_cols).astype(jnp.int32)
    end_count = line_node.shape[0]
    end_node = ((jnp.arange(end_count, dtype=jnp.int32) // (2 * LN)) * NODE_DEV + line_node).astype(jnp.int32)
    conv_global = (conv_region[:, 0] * NODE_DEV + conv_node).astype(jnp.int32)
    conductance = 0.25 * jnp.power(jnp.float32(2.0), fault_kind.astype(jnp.float32))
    scen_index = jnp.arange(SCEN, dtype=jnp.int32)
    delay_pick = (line_delay[None, :] == jnp.arange(1, DMAX + 1, dtype=jnp.int32)[:, None]).astype(jnp.float32)
    voltage = voltage_init
    branch = branch_init
    waves = wave_init
    filtered = conv_init[0]
    conv_amps = conv_init[1]
    envelope = jnp.zeros((NODES,), jnp.float32)
    for step_index in range(STEPS):
        drive = jnp.sum(delay_pick[:, None, :] * waves, axis=0)
        branch = node_decay[None, :] * branch + node_gain[None, :] * voltage
        measured = voltage[:, conv_global]
        filtered = filtered + conv_gains[1][None, :] * (measured - filtered)
        target_amps = conv_power[None, :] * filtered / (1.0 + filtered * filtered)
        conv_amps = conv_amps + conv_gains[0][None, :] * (target_amps - conv_amps)
        current = source_current[None, :] - branch
        current = current.at[:, end_node].add(drive)
        current = current.at[:, conv_global].add(conv_amps)
        current = current.at[scen_index, fault_node].add(-conductance * voltage[scen_index, fault_node])
        voltage = apply_inverse(inverse_blocks, global_cols, current)
        envelope = jnp.maximum(envelope, jnp.max(jnp.abs(voltage), axis=0))
        launch = 2.0 * line_admittance[None, :] * voltage[:, end_node] - drive
        split_ends = launch.reshape(SCEN, region_count, 2, LN)
        from_previous = jnp.roll(split_ends[:, :, 1, :], 1, axis=1)
        from_following = jnp.roll(split_ends[:, :, 0, :], -1, axis=1)
        arrived = jnp.stack([from_previous, from_following], axis=2).reshape(SCEN, end_count)
        waves = jnp.concatenate([arrived[None], waves[:-1]], axis=0)
    conv_state = jnp.stack([filtered, conv_amps], axis=0)
    return (voltage, branch, waves, conv_state, envelope)
```

```python
import functools

import jax
import jax.numpy as jnp
from jax import lax
from jax.experimental import pallas as pl
from jax.experimental.pallas import tpu as pltpu
from jax.sharding import PartitionSpec as P

STEPS = 4
BLK = 96
KB = 5
NB = 32
CAP = 14
ROWS = 16
LN = 128
DMAX = 8
MESH = pl.DeviceIdType.MESH
F32 = jnp.float32
BF16 = jnp.bfloat16


def lanes(shape, axis):
    return lax.broadcasted_iota(jnp.int32, shape, axis)


def low_half(shape):
    return lanes(shape, len(shape) - 1) % 128 < 64


def both(z):
    return z + pltpu.roll(z, 64, 1)


def split(x):
    lead = x.astype(BF16).astype(F32)
    return jnp.where(low_half(x.shape), lead, x - lead).astype(BF16)


def column(row):
    return jnp.broadcast_to(row, (128, 128)).T


def kernel(
    regions,
    scens,
    cols_ref,
    payload_ref,
    back_ref,
    vinit_ref,
    binit_ref,
    winit_ref,
    nodes_ref,
    lines_ref,
    fault_ref,
    blocks_ref,
    volt_out,
    branch_out,
    wave_out,
    conv_out,
    env_out,
    wraw,
    wmat,
    scat,
    gath,
    volt,
    branch,
    cur,
    env,
    decay,
    gain,
    source,
    xop,
    vop,
    aop,
    dop,
    drive,
    hist,
    state,
    ret,
    power,
    gamps,
    gfilt,
    ldelay,
    ladm,
    sendbuf,
    arrived,
    envbuf,
    load_sem,
    fsend,
    frecv,
    fself,
    bsend,
    brecv,
    bself,
    lsend,
    lrecv,
    esend,
    erecv,
):
    me = lax.axis_index("region")
    sc = lax.axis_index("scen")
    nxt = lax.rem(me + 1, regions)
    prv = lax.rem(me + regions - 1, regions)
    slots = regions * ROWS
    nodes = volt.shape[0]
    ctile = min(256, slots)

    barrier = pltpu.get_barrier_semaphore()

    def greet(k, _):
        pl.semaphore_signal(
            barrier, inc=1, device_id={"region": lax.rem(me + k, regions)}, device_id_type=MESH
        )
        return 0

    lax.fori_loop(1, regions, greet, 0)
    for k in range(1, scens):
        pl.semaphore_signal(
            barrier, inc=1, device_id={"scen": lax.rem(sc + k, scens)}, device_id_type=MESH
        )
    load = pltpu.make_async_copy(blocks_ref, wraw, load_sem)
    load.start()
    pl.semaphore_wait(barrier, regions - 1 + scens - 1)

    def forward(peer):
        return pltpu.make_async_remote_copy(
            src_ref=payload_ref.at[peer],
            dst_ref=state.at[me],
            send_sem=fsend.at[peer],
            recv_sem=frecv.at[me],
            device_id={"region": peer},
            device_id_type=MESH,
        )

    def backward(peer):
        return pltpu.make_async_remote_copy(
            src_ref=state.at[peer],
            dst_ref=ret.at[me],
            send_sem=bsend.at[peer],
            recv_sem=brecv.at[me],
            device_id={"region": peer},
            device_id_type=MESH,
        )

    def start_forward(k, _):
        forward(lax.rem(me + k, regions)).start()
        return 0

    lax.fori_loop(1, regions, start_forward, 0)
    own = pltpu.make_async_copy(payload_ref.at[me], state.at[me], fself)
    own.start()

    def place(c, _):
        at = pl.ds(pl.multiple_of(c * 128, 128), 128)
        v = vinit_ref[:, at]
        v = jnp.concatenate([v, v], axis=0).T
        volt[at, :] = v
        vop[at, :] = split(v)
        b = binit_ref[:, at]
        branch[at, :] = jnp.concatenate([b, b], axis=0).T
        decay[at, :] = column(nodes_ref[0, pl.ds(c, 1), :])
        gain[at, :] = column(nodes_ref[1, pl.ds(c, 1), :])
        source[at, :] = column(nodes_ref[2, pl.ds(c, 1), :])
        env[at, :] = jnp.zeros((128, 128), F32)
        return 0

    lax.fori_loop(0, nodes // 128, place, 0)

    def place_wave(d, _):
        for h in range(2):
            w = winit_ref[d, :, h * 128 : h * 128 + 128]
            hist[DMAX - 1 - d, h * 128 : h * 128 + 128, :] = jnp.concatenate([w, w], axis=0).T
        return 0

    lax.fori_loop(0, DMAX, place_wave, 0)

    for h in range(2):
        at = slice(h * 128, h * 128 + 128)
        ldelay[at, :] = column(lines_ref[1, h : h + 1, :])
        ladm[at, :] = 2.0 * column(lines_ref[2, h : h + 1, :])
        lnode = column(lines_ref[0, h : h + 1, :])

        def line_gather(c, _):
            here = (lanes((128, 128), 1) + c * 128).astype(F32)
            gath[slots + h * 128 : slots + h * 128 + 128, pl.ds(pl.multiple_of(c * 128, 128), 128)] = (
                jnp.where(lnode == here, 1.0, 0.0).astype(BF16)
            )
            return 0

        lax.fori_loop(0, nodes // 128, line_gather, 0)

        def line_scatter(c, _):
            here = (lanes((128, 128), 0) + c * 128).astype(F32)
            row = lines_ref[0, h : h + 1, :]
            scat[pl.ds(pl.multiple_of(c * 128, 128), 128), slots + h * 128 : slots + h * 128 + 128] = (
                jnp.where(row == here, 1.0, 0.0).astype(BF16)
            )
            return 0

        lax.fori_loop(0, nodes // 128, line_scatter, 0)

    load.wait()

    def prepare(b, _):
        parts = [wraw[b, k] for k in range(KB)]
        whole = jnp.concatenate(parts + [jnp.zeros((BLK, 512 - KB * BLK), F32)], axis=1)
        lead = whole.astype(BF16)
        wmat[b, 0:BLK, :] = lead
        wmat[b, BLK : 2 * BLK, :] = (whole - lead.astype(F32)).astype(BF16)
        return 0

    lax.fori_loop(0, NB, prepare, 0)

    own.wait()

    def wait_forward(k, _):
        forward(lax.rem(me + k, regions)).wait_send()
        return 0

    lax.fori_loop(1, regions, wait_forward, 0)

    def arrive_forward(k, _):
        frm = lax.rem(me + regions - k, regions)
        pltpu.make_async_remote_copy(
            src_ref=payload_ref.at[frm],
            dst_ref=state.at[frm],
            send_sem=fsend.at[frm],
            recv_sem=frecv.at[frm],
            device_id={"region": frm},
            device_id_type=MESH,
        ).wait_recv()
        return 0

    lax.fori_loop(1, regions, arrive_forward, 0)

    params = state[:, CAP, :]
    lead = params.astype(BF16).astype(F32)
    lane64 = lanes((regions, 128), 1) < 64
    pair = jnp.where(lane64, lead, pltpu.roll(params - lead, 64, 1))
    fold = (lanes((128, slots), 0) % 64 == lanes((128, slots), 1) % ROWS).astype(F32).astype(BF16)
    spread = jnp.dot(pair.astype(BF16), fold, preferred_element_type=F32)
    mine = lanes((regions, slots), 0) == lanes((regions, slots), 1) // ROWS
    noderow = jnp.sum(jnp.where(mine, spread, 0.0), axis=0, keepdims=True)

    def conv_scatter(c, _):
        here = (lanes((128, slots), 0) + (c * 128 + 1)).astype(F32)
        scat[pl.ds(pl.multiple_of(c * 128, 128), 128), 0:slots] = (
            jnp.where(noderow == here, 1.0, 0.0).astype(BF16)
        )
        return 0

    lax.fori_loop(0, nodes // 128, conv_scatter, 0)

    pick = ((lanes((128, 512), 0) % 64) // ROWS == lanes((128, 512), 1) // 128).astype(F32).astype(BF16)

    def conv_param(i, _):
        r0 = i * (ctile // ROWS)
        prm = state[pl.ds(r0, ctile // ROWS), CAP, :]
        ld = prm.astype(BF16).astype(F32)
        both_parts = jnp.where(low_half(prm.shape), ld, pltpu.roll(prm - ld, 64, 1))
        rep = jnp.broadcast_to(both_parts[:, None, :], (ctile // ROWS, ROWS, 128)).reshape(ctile, 128)
        slot = lanes((ctile, 128), 0) % ROWS
        rep = jnp.where(lanes((ctile, 128), 1) % ROWS == slot, rep, 0.0).astype(BF16)
        got = jnp.dot(rep, pick, preferred_element_type=F32)
        at = pl.ds(pl.multiple_of(i * ctile, ctile), ctile)
        node = got[:, 0:128]
        power[at, :] = got[:, 128:256]
        gamps[at, :] = got[:, 256:384]
        gfilt[at, :] = got[:, 384:512]
        for c in range(nodes // 128):
            here = (lanes((ctile, 128), 1) + (c * 128 + 1)).astype(F32)
            gath[at, c * 128 : c * 128 + 128] = jnp.where(node == here, 1.0, 0.0).astype(BF16)
        return 0

    lax.fori_loop(0, slots // ctile, conv_param, 0)

    fault = fault_ref[0:1, :]
    conduct = fault_ref[1:2, :]

    def line_copies(t):
        return [
            pltpu.make_async_remote_copy(
                src_ref=sendbuf.at[t, side],
                dst_ref=arrived.at[t, side],
                send_sem=lsend.at[t, side],
                recv_sem=lrecv.at[t, side],
                device_id={"region": to},
                device_id_type=MESH,
            )
            for side, to in ((0, nxt), (1, prv))
        ]

    def take_arrivals(t):
        for side, copy in enumerate(line_copies(t)):
            copy.wait()
            p = arrived[t, side]
            q = pltpu.roll(p, 64, 1)
            low = low_half(p.shape)
            hist[DMAX + t, side * LN : side * LN + 64, :] = jnp.where(low, p, q)
            hist[DMAX + t, side * LN + 64 : side * LN + 128, :] = jnp.where(low, q, p)

    def step(t, last):
        def conv(i, _):
            at = pl.ds(pl.multiple_of(i * ctile, ctile), ctile)
            m = both(jnp.dot(gath[at, :], vop[...], preferred_element_type=F32))
            rows = pl.ds(i * (ctile // ROWS), ctile // ROWS)
            f = state[rows].reshape(ctile, 128)
            low = low_half(f.shape)
            filt = f + gfilt[at, :] * (m - f)
            full = jnp.where(low, filt, pltpu.roll(filt, 64, 1))
            goal = power[at, :] * full / (1.0 + full * full)
            amps = f + gamps[at, :] * (goal - f)
            state[rows] = jnp.where(low, filt, amps).reshape(ctile // ROWS, ROWS, 128)
            aop[at, :] = split(jnp.where(low, pltpu.roll(amps, 64, 1), amps))
            return 0

        lax.fori_loop(0, slots // ctile, conv, 0)

        if last:

            def start_backward(k, _):
                backward(lax.rem(me + k, regions)).start()
                return 0

            lax.fori_loop(1, regions, start_backward, 0)
            pltpu.make_async_copy(state.at[me], ret.at[me], bself).start()

        def gather_current(i, _):
            at = pl.ds(pl.multiple_of(i * 256, 256), 256)
            z = both(jnp.dot(scat[at, 0:slots], aop[...], preferred_element_type=F32))
            v = volt[at, :]
            b = decay[at, :] * branch[at, :] + gain[at, :] * v
            branch[at, :] = b
            here = lanes((256, 128), 0) + i * 256
            hit = jnp.where(fault == here.astype(F32), conduct * v, 0.0)
            cur[at, :] = source[at, :] - b - hit + z
            return 0

        lax.fori_loop(0, nodes // 256, gather_current, 0)

        if t > 0:
            take_arrivals(t - 1)
        d = jnp.zeros((2 * LN, 128), F32)
        for k in range(1, DMAX + 1):
            d = d + jnp.where(ldelay[...] == float(k), hist[DMAX + t - k], 0.0)
        drive[...] = d
        dop[...] = split(d)

        def add_lines(i, _):
            at = pl.ds(pl.multiple_of(i * 4 * BLK, 4 * BLK), 4 * BLK)
            z = both(jnp.dot(scat[at, slots : slots + 2 * LN], dop[...], preferred_element_type=F32))
            x = split(cur[at, :] + z)
            for q in range(4):
                xop[4 * i + q] = x[q * BLK : (q + 1) * BLK]
            return 0

        lax.fori_loop(0, nodes // (4 * BLK), add_lines, 0)

        def solve(b, _):
            parts = [xop[cols_ref[b, k]] for k in range(KB)]
            x = jnp.concatenate(parts + [jnp.zeros((512 - KB * BLK, 128), BF16)], axis=0)
            z = jnp.dot(wmat[b], x, preferred_element_type=F32)
            v = both(z[0:BLK] + z[BLK : 2 * BLK])
            at = pl.ds(pl.multiple_of(b * BLK, BLK), BLK)
            volt[at, :] = v
            vop[at, :] = split(v)
            env[at, :] = jnp.maximum(env[at, :], jnp.abs(v))
            return 0

        lax.fori_loop(0, NB, solve, 0)

        ends = both(jnp.dot(gath[slots : slots + 2 * LN, :], vop[...], preferred_element_type=F32))
        launch = ladm[...] * ends - drive[...]
        low = low_half((64, 128))
        sendbuf[t, 0] = jnp.where(low, launch[LN : LN + 64], launch[LN + 64 : 2 * LN])
        sendbuf[t, 1] = jnp.where(low, launch[0:64], launch[64:LN])
        for copy in line_copies(t):
            copy.start()

    for t in range(STEPS):
        step(t, t == STEPS - 1)

    def peak(c, _):
        at = pl.ds(pl.multiple_of(c * 128, 128), 128)
        envbuf[sc, pl.ds(c, 1), :] = jnp.max(env[at, :].T, axis=0, keepdims=True)
        return 0

    lax.fori_loop(0, nodes // 128, peak, 0)

    def env_copy(k):
        return pltpu.make_async_remote_copy(
            src_ref=envbuf.at[sc],
            dst_ref=envbuf.at[sc],
            send_sem=esend.at[k],
            recv_sem=erecv.at[k],
            device_id={"scen": lax.rem(sc + k, scens)},
            device_id_type=MESH,
        )

    for k in range(1, scens):
        env_copy(k).start()

    def finish(c, _):
        at = pl.ds(pl.multiple_of(c * 128, 128), 128)
        volt_out[:, at] = volt[at, :].T[0:64]
        branch_out[:, at] = branch[at, :].T[0:64]
        return 0

    lax.fori_loop(0, nodes // 128, finish, 0)

    take_arrivals(STEPS - 1)
    for j in range(STEPS):
        for h in range(2):
            at = slice(h * 128, h * 128 + 128)
            wave_out[j, :, at] = hist[DMAX + STEPS - 1 - j, at, :].T[0:64]
    for j in range(STEPS, DMAX):
        wave_out[j] = winit_ref[j - STEPS]

    pltpu.make_async_copy(state.at[me], ret.at[me], bself).wait()

    def wait_backward(k, _):
        backward(lax.rem(me + k, regions)).wait_send()
        return 0

    lax.fori_loop(1, regions, wait_backward, 0)

    def arrive_backward(k, _):
        frm = lax.rem(me + regions - k, regions)
        pltpu.make_async_remote_copy(
            src_ref=state.at[frm],
            dst_ref=ret.at[frm],
            send_sem=bsend.at[frm],
            recv_sem=brecv.at[frm],
            device_id={"region": frm},
            device_id_type=MESH,
        ).wait_recv()
        return 0

    lax.fori_loop(1, regions, arrive_backward, 0)

    r = ret[...].reshape(slots, 128)
    lead = r.astype(BF16)
    rest = (r - lead.astype(F32)).astype(BF16)
    got = jnp.dot(back_ref[...], jnp.concatenate([lead, rest], axis=1), preferred_element_type=F32)
    got = got[:, 0:128] + got[:, 128:256]
    for c in range(got.shape[0] // 128):
        tile = got[c * 128 : c * 128 + 128].T
        conv_out[0, :, c * 128 : c * 128 + 128] = tile[0:64]
        conv_out[1, :, c * 128 : c * 128 + 128] = tile[64:128]

    for k in range(1, scens):
        env_copy(k).wait()
    best = envbuf[0]
    for k in range(1, scens):
        best = jnp.maximum(best, envbuf[k])
    env_out[...] = best


def shards(
    regions,
    scens,
    inverse_blocks,
    block_cols,
    source_current,
    node_decay,
    node_gain,
    voltage_init,
    branch_init,
    wave_init,
    line_node,
    line_delay,
    line_admittance,
    conv_region,
    conv_node,
    conv_power,
    conv_gains,
    conv_init,
    fault_node,
    fault_kind,
):
    scen_count, nodes = voltage_init.shape
    convs = conv_node.shape[0]
    slots = regions * ROWS
    hi = lax.Precision.HIGHEST

    target = conv_region[:, 0]
    member = (target[:, None] == jnp.arange(regions, dtype=jnp.int32)[None, :]).astype(F32)
    index = jnp.arange(convs, dtype=jnp.int32)
    before = (index[:, None] > index[None, :]).astype(BF16)
    earlier = jnp.dot(before, member.astype(BF16), preferred_element_type=F32)
    rank = jnp.sum(earlier * member, axis=1).astype(jnp.int32)
    position = target * ROWS + rank
    slot = jnp.arange(slots, dtype=jnp.int32)
    there = (slot[:, None] == position[None, :]).astype(F32)
    back = (position[:, None] == slot[None, :]).astype(BF16)
    content = lax.dot_general(
        there, conv_init.reshape(2 * scen_count, convs), (((1,), (1,)), ((), ())), precision=hi
    )
    prm = jnp.stack([conv_node.astype(F32) + 1.0, conv_power, conv_gains[0], conv_gains[1]])
    prm = lax.dot_general(prm, there, (((1,), (1,)), ((), ())), precision=hi)
    prm = prm.reshape(4, regions, ROWS).transpose(1, 0, 2).reshape(regions, 4 * ROWS)
    prm = jnp.concatenate([prm, jnp.zeros((regions, 64), F32)], axis=1)
    payload = content.reshape(regions, ROWS, 128)
    at_params = jnp.arange(ROWS, dtype=jnp.int32)[None, :, None] == CAP
    payload = jnp.where(at_params, prm[:, None, :], payload)

    tiles = nodes // 128
    node_rows = jnp.stack(
        [node_decay.reshape(tiles, 128), node_gain.reshape(tiles, 128), source_current.reshape(tiles, 128)]
    )
    line_rows = jnp.stack(
        [
            line_node.reshape(2, LN).astype(F32),
            line_delay.reshape(2, LN).astype(F32),
            line_admittance.reshape(2, LN),
        ]
    )
    local = fault_node - lax.axis_index("region") * nodes
    conduct = 0.25 * jnp.left_shift(1, fault_kind).astype(F32)
    local = local.astype(F32)
    fault_rows = jnp.stack([jnp.concatenate([local, local]), jnp.concatenate([conduct, conduct])])

    vm = pl.BlockSpec(memory_space=pltpu.VMEM)
    wide = pltpu.VMEM((nodes, 128), F32)
    dma = pltpu.SemaphoreType.DMA
    volt, branch, wave, conv, env = pl.pallas_call(
        functools.partial(kernel, regions, scens),
        out_shape=(
            jax.ShapeDtypeStruct(voltage_init.shape, F32),
            jax.ShapeDtypeStruct(voltage_init.shape, F32),
            jax.ShapeDtypeStruct(wave_init.shape, F32),
            jax.ShapeDtypeStruct(conv_init.shape, F32),
            jax.ShapeDtypeStruct((tiles, 128), F32),
        ),
        in_specs=[pl.BlockSpec(memory_space=pltpu.SMEM)] + [vm] * 8 + [pl.BlockSpec(memory_space=pl.ANY)],
        out_specs=(vm,) * 5,
        scratch_shapes=[
            pltpu.VMEM((NB, KB, BLK, BLK), F32),
            pltpu.VMEM((NB, 2 * BLK, 512), BF16),
            pltpu.VMEM((nodes, slots + 2 * LN), BF16),
            pltpu.VMEM((slots + 2 * LN, nodes), BF16),
            wide,
            wide,
            wide,
            wide,
            wide,
            wide,
            wide,
            pltpu.VMEM((NB, BLK, 128), BF16),
            pltpu.VMEM((nodes, 128), BF16),
            pltpu.VMEM((slots, 128), BF16),
            pltpu.VMEM((2 * LN, 128), BF16),
            pltpu.VMEM((2 * LN, 128), F32),
            pltpu.VMEM((DMAX + STEPS, 2 * LN, 128), F32),
            pltpu.VMEM((regions, ROWS, 128), F32),
            pltpu.VMEM((regions, ROWS, 128), F32),
            pltpu.VMEM((slots, 128), F32),
            pltpu.VMEM((slots, 128), F32),
            pltpu.VMEM((slots, 128), F32),
            pltpu.VMEM((2 * LN, 128), F32),
            pltpu.VMEM((2 * LN, 128), F32),
            pltpu.VMEM((STEPS, 2, 64, 128), F32),
            pltpu.VMEM((STEPS, 2, 64, 128), F32),
            pltpu.VMEM((scens, tiles, 128), F32),
            dma,
            dma((regions,)),
            dma((regions,)),
            dma,
            dma((regions,)),
            dma((regions,)),
            dma,
            dma((STEPS, 2)),
            dma((STEPS, 2)),
            dma((scens,)),
            dma((scens,)),
        ],
        compiler_params=pltpu.CompilerParams(
            collective_id=0, has_side_effects=True, vmem_limit_bytes=67043328
        ),
        name="transient",
    )(
        block_cols,
        payload,
        back,
        voltage_init,
        branch_init,
        wave_init,
        node_rows,
        line_rows,
        fault_rows,
        inverse_blocks,
    )
    return (volt, branch, wave, conv, env.reshape(nodes))


def solution(mesh):
    placed = (
        P("region", None, None, None),
        P("region", None),
        P("region"),
        P("region"),
        P("region"),
        P("scen", "region"),
        P("scen", "region"),
        P(None, "scen", "region"),
        P("region"),
        P("region"),
        P("region"),
        P("region", None),
        P("region"),
        P("region"),
        P(None, "region"),
        P(None, "scen", "region"),
        P("scen"),
        P("scen"),
    )
    return jax.shard_map(
        functools.partial(shards, mesh.shape["region"], mesh.shape["scen"]),
        mesh=mesh,
        in_specs=placed,
        out_specs=(
            P("scen", "region"),
            P("scen", "region"),
            P(None, "scen", "region"),
            P(None, "scen", "region"),
            P("region"),
        ),
        check_vma=False,
    )
```

```python
import functools

import jax
import jax.numpy as jnp
from jax import lax
from jax.experimental import pallas as pl
from jax.experimental.pallas import tpu as pltpu
from jax.sharding import PartitionSpec as P

STEPS = 4
BLK = 96
KB = 5
NB = 32
CAP = 14
ROWS = 16
LN = 128
DMAX = 8
NTILE = 1536
GROUP = 16
MESH = pl.DeviceIdType.MESH
F32 = jnp.float32
BF16 = jnp.bfloat16


def lanes(shape, axis):
    return lax.broadcasted_iota(jnp.int32, shape, axis)


def low_half(shape):
    return lanes(shape, len(shape) - 1) % 128 < 64


def both(z):
    return z + pltpu.roll(z, 64, 1)


def split(x):
    lead = x.astype(BF16).astype(F32)
    return jnp.where(low_half(x.shape), lead, x - lead).astype(BF16)


def column(row):
    return jnp.broadcast_to(row, (128, 128)).T


def kernel(
    regions,
    scens,
    blocks_ref,
    cols_ref,
    ends_ref,
    vinit_ref,
    binit_ref,
    winit_ref,
    cinit_ref,
    decay_ref,
    gain_ref,
    source_ref,
    lnode_ref,
    ldelay_ref,
    ladm_ref,
    region_ref,
    cnode_ref,
    cpower_ref,
    cgains_ref,
    fnode_ref,
    fkind_ref,
    volt_out,
    branch_out,
    wave_out,
    conv_out,
    env_out,
    payload_ref,
    back_ref,
    wraw,
    wmat,
    scat,
    volt,
    branch,
    env,
    decay,
    gain,
    source,
    xop,
    aop,
    measured,
    ends,
    indexv,
    index,
    drive,
    hist,
    state,
    ret,
    power,
    gamps,
    gfilt,
    ldelay,
    ladm,
    sendbuf,
    arrived,
    envbuf,
    load_sem,
    index_sem,
    fsend,
    frecv,
    fself,
    bsend,
    brecv,
    bself,
    lsend,
    lrecv,
    esend,
    erecv,
):
    me = lax.axis_index("region")
    sc = lax.axis_index("scen")
    nxt = lax.rem(me + 1, regions)
    prv = lax.rem(me + regions - 1, regions)
    slots = regions * ROWS
    nodes = volt.shape[0]
    ctile = min(256, slots)
    pairs = 128 // ROWS

    barrier = pltpu.get_barrier_semaphore()

    def greet(k, _):
        pl.semaphore_signal(
            barrier, inc=1, device_id={"region": lax.rem(me + k, regions)}, device_id_type=MESH
        )
        return 0

    lax.fori_loop(1, regions, greet, 0)
    for k in range(1, scens):
        pl.semaphore_signal(
            barrier, inc=1, device_id={"scen": lax.rem(sc + k, scens)}, device_id_type=MESH
        )
    load = pltpu.make_async_copy(blocks_ref, wraw, load_sem)
    load.start()

    convs = back_ref.shape[0]
    lane = lanes((convs, 128), 1)
    target = jnp.concatenate(
        [column(region_ref[:, h * 128 : h * 128 + 128].astype(F32)) for h in range(convs // 128)], axis=0
    )
    member = jnp.where(target == lane.astype(F32), 1.0, 0.0)
    before = jnp.where(lanes((convs, convs), 0) > lanes((convs, convs), 1), 1.0, 0.0)
    earlier = jnp.dot(before.astype(BF16), member.astype(BF16), preferred_element_type=F32)
    rank = jnp.sum(earlier * member, axis=1, keepdims=True)
    position = target * float(ROWS) + rank
    for c in range(slots // 128):
        back_ref[:, c * 128 : c * 128 + 128] = jnp.where(
            position == (lane + c * 128).astype(F32), 1.0, 0.0
        ).astype(BF16)
    content = jnp.concatenate([cinit_ref[0], cinit_ref[1]], axis=0)
    lead = content.astype(BF16)
    rest = (content - lead.astype(F32)).astype(BF16)
    content = jnp.dot(
        jnp.concatenate([lead, rest], axis=0), back_ref[...], preferred_element_type=F32
    )
    content = content[0:128] + content[128:256]
    for c in range(slots // 128):
        payload_ref[c * pairs : c * pairs + pairs] = content[:, c * 128 : c * 128 + 128].T.reshape(
            pairs, ROWS, 128
        )
    params = jnp.concatenate(
        [
            jnp.concatenate(
                [
                    cnode_ref[h : h + 1, :].astype(F32) + 1.0,
                    cpower_ref[h : h + 1, :],
                    cgains_ref[:, h * 128 : h * 128 + 128],
                    jnp.zeros((124, 128), F32),
                ],
                axis=0,
            ).T
            for h in range(convs // 128)
        ],
        axis=0,
    )
    values = jnp.zeros((convs, 128), F32)
    for w in range(4):
        values = values + jnp.where(lane // ROWS == w, params[:, w : w + 1], 0.0)
    values = jnp.where((lane % ROWS).astype(F32) == rank, values, 0.0)
    lead = values.astype(BF16).astype(F32)
    values = jnp.where(lane < 64, lead, pltpu.roll(values - lead, 64, 1)).astype(BF16)
    owners = jnp.concatenate(
        [member[h * 128 : h * 128 + 128].T for h in range(convs // 128)], axis=1
    ).astype(BF16)
    payload_ref[:, CAP, :] = both(jnp.dot(owners, values, preferred_element_type=F32))[0:regions]

    pl.semaphore_wait(barrier, regions - 1 + scens - 1)

    def forward(peer):
        return pltpu.make_async_remote_copy(
            src_ref=payload_ref.at[peer],
            dst_ref=state.at[me],
            send_sem=fsend.at[peer],
            recv_sem=frecv.at[me],
            device_id={"region": peer},
            device_id_type=MESH,
        )

    def backward(peer):
        return pltpu.make_async_remote_copy(
            src_ref=state.at[peer],
            dst_ref=ret.at[me],
            send_sem=bsend.at[peer],
            recv_sem=brecv.at[me],
            device_id={"region": peer},
            device_id_type=MESH,
        )

    def start_forward(k, _):
        forward(lax.rem(me + k, regions)).start()
        return 0

    lax.fori_loop(1, regions, start_forward, 0)
    own = pltpu.make_async_copy(payload_ref.at[me], state.at[me], fself)
    own.start()

    def place(c, _):
        at = pl.ds(pl.multiple_of(c * 128, 128), 128)
        v = vinit_ref[:, at]
        v = jnp.concatenate([v, v], axis=0).T
        volt[at, :] = v
        b = binit_ref[:, at]
        branch[at, :] = jnp.concatenate([b, b], axis=0).T
        decay[at, :] = column(decay_ref[pl.ds(c, 1), :])
        gain[at, :] = column(gain_ref[pl.ds(c, 1), :])
        source[at, :] = column(source_ref[pl.ds(c, 1), :])
        env[at, :] = jnp.zeros((128, 128), F32)
        return 0

    lax.fori_loop(0, nodes // 128, place, 0)

    def place_wave(d, _):
        for h in range(2):
            w = winit_ref[d, :, h * 128 : h * 128 + 128]
            hist[DMAX - 1 - d, h * 128 : h * 128 + 128, :] = jnp.concatenate([w, w], axis=0).T
        return 0

    lax.fori_loop(0, DMAX, place_wave, 0)

    for h in range(2):
        at = slice(h * 128, h * 128 + 128)
        ldelay[at, :] = column(ldelay_ref[h : h + 1, :].astype(F32))
        ladm[at, :] = 2.0 * column(ladm_ref[h : h + 1, :])
        def line_scatter(c, _):
            here = (lanes((128, 128), 0) + c * 128).astype(F32)
            row = lnode_ref[h : h + 1, :].astype(F32)
            scat[pl.ds(pl.multiple_of(c * 128, 128), 128), slots + h * 128 : slots + h * 128 + 128] = (
                jnp.where(row == here, 1.0, 0.0).astype(BF16)
            )
            return 0

        lax.fori_loop(0, nodes // 128, line_scatter, 0)

    load.wait()

    def prepare(b, _):
        parts = [wraw[b, k] for k in range(KB)]
        whole = jnp.concatenate(parts + [jnp.zeros((BLK, 512 - KB * BLK), F32)], axis=1)
        lead = whole.astype(BF16)
        wmat[b, 0:BLK, :] = lead
        wmat[b, BLK : 2 * BLK, :] = (whole - lead.astype(F32)).astype(BF16)
        return 0

    lax.fori_loop(0, NB, prepare, 0)

    own.wait()

    def wait_forward(k, _):
        forward(lax.rem(me + k, regions)).wait_send()
        return 0

    lax.fori_loop(1, regions, wait_forward, 0)

    def arrive_forward(k, _):
        frm = lax.rem(me + regions - k, regions)
        pltpu.make_async_remote_copy(
            src_ref=payload_ref.at[frm],
            dst_ref=state.at[frm],
            send_sem=fsend.at[frm],
            recv_sem=frecv.at[frm],
            device_id={"region": frm},
            device_id_type=MESH,
        ).wait_recv()
        return 0

    lax.fori_loop(1, regions, arrive_forward, 0)

    params = state[:, CAP, :]
    lead = params.astype(BF16).astype(F32)
    lane64 = lanes((regions, 128), 1) < 64
    pair = jnp.where(lane64, lead, pltpu.roll(params - lead, 64, 1))
    fold = (lanes((128, slots), 0) % 64 == lanes((128, slots), 1) % ROWS).astype(F32).astype(BF16)
    spread = jnp.dot(pair.astype(BF16), fold, preferred_element_type=F32)
    mine = lanes((regions, slots), 0) == lanes((regions, slots), 1) // ROWS
    noderow = jnp.sum(jnp.where(mine, spread, 0.0), axis=0, keepdims=True)

    for r in range(slots // 128):
        number = noderow[:, r * 128 : r * 128 + 128].astype(jnp.int32) - 1
        indexv[r : r + 1, :] = jnp.clip(number, 0, nodes - 1)
    to_scalars = pltpu.make_async_copy(indexv, index, index_sem)
    to_scalars.start()

    def conv_scatter(c, _):
        here = (lanes((128, slots), 0) + (c * 128 + 1)).astype(F32)
        scat[pl.ds(pl.multiple_of(c * 128, 128), 128), 0:slots] = (
            jnp.where(noderow == here, 1.0, 0.0).astype(BF16)
        )
        return 0

    lax.fori_loop(0, nodes // 128, conv_scatter, 0)

    pick = ((lanes((128, 384), 0) % 64) // ROWS == lanes((128, 384), 1) // 128 + 1).astype(F32).astype(BF16)

    def conv_param(i, _):
        r0 = i * (ctile // ROWS)
        prm = state[pl.ds(r0, ctile // ROWS), CAP, :]
        ld = prm.astype(BF16).astype(F32)
        both_parts = jnp.where(low_half(prm.shape), ld, pltpu.roll(prm - ld, 64, 1))
        rep = jnp.broadcast_to(both_parts[:, None, :], (ctile // ROWS, ROWS, 128)).reshape(ctile, 128)
        slot = lanes((ctile, 128), 0) % ROWS
        rep = jnp.where(lanes((ctile, 128), 1) % ROWS == slot, rep, 0.0).astype(BF16)
        got = jnp.dot(rep, pick, preferred_element_type=F32)
        at = pl.ds(pl.multiple_of(i * ctile, ctile), ctile)
        power[at, :] = got[:, 0:128]
        gamps[at, :] = got[:, 128:256]
        gfilt[at, :] = got[:, 256:384]
        return 0

    lax.fori_loop(0, slots // ctile, conv_param, 0)

    measured[...] = jnp.zeros_like(measured)
    to_scalars.wait()
    fault = (fnode_ref[...] - me * nodes).astype(F32)
    fault = jnp.concatenate([fault, fault], axis=1)
    conduct = 0.25 * jnp.left_shift(1, fkind_ref[...]).astype(F32)
    conduct = jnp.concatenate([conduct, conduct], axis=1)

    def line_copies(t):
        return [
            pltpu.make_async_remote_copy(
                src_ref=sendbuf.at[t, side],
                dst_ref=arrived.at[t, side],
                send_sem=lsend.at[t, side],
                recv_sem=lrecv.at[t, side],
                device_id={"region": to},
                device_id_type=MESH,
            )
            for side, to in ((0, nxt), (1, prv))
        ]

    def take_arrivals(t):
        for side, copy in enumerate(line_copies(t)):
            copy.wait()
            p = arrived[t, side]
            q = pltpu.roll(p, 64, 1)
            low = low_half(p.shape)
            hist[DMAX + t, side * LN : side * LN + 64, :] = jnp.where(low, p, q)
            hist[DMAX + t, side * LN + 64 : side * LN + 128, :] = jnp.where(low, q, p)

    def step(t, last):
        def conv(i, _):
            for q in range(pairs):
                for j in range(CAP):
                    measured[pl.ds(i * 128 + q * ROWS + j, 1), :] = volt[jnp.clip(index[i, q * ROWS + j], 0, nodes - 1)][None]
            at = pl.ds(pl.multiple_of(i * 128, 128), 128)
            m = measured[at, :]
            rows = pl.ds(i * pairs, pairs)
            f = state[rows].reshape(128, 128)
            low = low_half(f.shape)
            filt = f + gfilt[at, :] * (m - f)
            full = jnp.where(low, filt, pltpu.roll(filt, 64, 1))
            goal = power[at, :] * full / (1.0 + full * full)
            amps = f + gamps[at, :] * (goal - f)
            state[rows] = jnp.where(low, filt, amps).reshape(pairs, ROWS, 128)
            aop[at, :] = split(jnp.where(low, pltpu.roll(amps, 64, 1), amps))
            return 0

        lax.fori_loop(0, slots // 128, conv, 0)

        if last:

            def start_backward(k, _):
                backward(lax.rem(me + k, regions)).start()
                return 0

            lax.fori_loop(1, regions, start_backward, 0)
            pltpu.make_async_copy(state.at[me], ret.at[me], bself).start()

        if t > 0:
            take_arrivals(t - 1)
        d = jnp.zeros((2 * LN, 128), F32)
        for k in range(1, DMAX + 1):
            d = d + jnp.where(ldelay[...] == float(k), hist[DMAX + t - k], 0.0)
        drive[...] = d
        aop[slots : slots + 2 * LN, :] = split(d)

        def assemble(i, _):
            at = pl.ds(pl.multiple_of(i * NTILE, NTILE), NTILE)
            z = both(jnp.dot(scat[at, :], aop[...], preferred_element_type=F32))
            v = volt[at, :]
            b = decay[at, :] * branch[at, :] + gain[at, :] * v
            branch[at, :] = b
            here = (lanes((NTILE, 128), 0) + i * NTILE).astype(F32)
            hit = jnp.where(fault == here, conduct * v, 0.0)
            x = split(source[at, :] - b - hit + z)
            for q in range(NTILE // BLK):
                xop[NTILE // BLK * i + q] = x[q * BLK : (q + 1) * BLK]
            return 0

        lax.fori_loop(0, nodes // NTILE, assemble, 0)

        def solve(i, _):
            found = []
            for q in range(GROUP):
                b = i * GROUP + q
                parts = [xop[cols_ref[k, b]] for k in range(KB)]
                x = jnp.concatenate(parts + [jnp.zeros((512 - KB * BLK, 128), BF16)], axis=0)
                z = jnp.dot(wmat[b], x, preferred_element_type=F32)
                found.append(both(z[0:BLK] + z[BLK : 2 * BLK]))
            at = pl.ds(pl.multiple_of(i * (GROUP * BLK), GROUP * BLK), GROUP * BLK)
            v = jnp.concatenate(found, axis=0)
            volt[at, :] = v
            env[at, :] = jnp.maximum(env[at, :], jnp.abs(v))
            return 0

        lax.fori_loop(0, NB // GROUP, solve, 0)

        def take_ends(i, _):
            for j in range(LN):
                ends[pl.ds(i * LN + j, 1), :] = volt[ends_ref[i, j]][None]
            return 0

        lax.fori_loop(0, 2, take_ends, 0)
        launch = ladm[...] * ends[...] - drive[...]
        low = low_half((64, 128))
        sendbuf[t, 0] = jnp.where(low, launch[LN : LN + 64], launch[LN + 64 : 2 * LN])
        sendbuf[t, 1] = jnp.where(low, launch[0:64], launch[64:LN])
        for copy in line_copies(t):
            copy.start()

    for t in range(STEPS):
        step(t, t == STEPS - 1)

    def peak(c, _):
        at = pl.ds(pl.multiple_of(c * 128, 128), 128)
        envbuf[sc, pl.ds(c, 1), :] = jnp.max(env[at, :].T, axis=0, keepdims=True)
        return 0

    lax.fori_loop(0, nodes // 128, peak, 0)

    def env_copy(k):
        return pltpu.make_async_remote_copy(
            src_ref=envbuf.at[sc],
            dst_ref=envbuf.at[sc],
            send_sem=esend.at[k],
            recv_sem=erecv.at[k],
            device_id={"scen": lax.rem(sc + k, scens)},
            device_id_type=MESH,
        )

    for k in range(1, scens):
        env_copy(k).start()

    def finish(c, _):
        at = pl.ds(pl.multiple_of(c * 128, 128), 128)
        volt_out[:, at] = volt[at, :].T[0:64]
        branch_out[:, at] = branch[at, :].T[0:64]
        return 0

    lax.fori_loop(0, nodes // 128, finish, 0)

    take_arrivals(STEPS - 1)
    for j in range(STEPS):
        for h in range(2):
            at = slice(h * 128, h * 128 + 128)
            wave_out[j, :, at] = hist[DMAX + STEPS - 1 - j, at, :].T[0:64]
    for j in range(STEPS, DMAX):
        wave_out[j] = winit_ref[j - STEPS]

    pltpu.make_async_copy(state.at[me], ret.at[me], bself).wait()

    def wait_backward(k, _):
        backward(lax.rem(me + k, regions)).wait_send()
        return 0

    lax.fori_loop(1, regions, wait_backward, 0)

    def arrive_backward(k, _):
        frm = lax.rem(me + regions - k, regions)
        pltpu.make_async_remote_copy(
            src_ref=state.at[frm],
            dst_ref=ret.at[frm],
            send_sem=bsend.at[frm],
            recv_sem=brecv.at[frm],
            device_id={"region": frm},
            device_id_type=MESH,
        ).wait_recv()
        return 0

    lax.fori_loop(1, regions, arrive_backward, 0)

    r = ret[...].reshape(slots, 128)
    lead = r.astype(BF16)
    rest = (r - lead.astype(F32)).astype(BF16)
    got = jnp.dot(back_ref[...], jnp.concatenate([lead, rest], axis=1), preferred_element_type=F32)
    got = got[:, 0:128] + got[:, 128:256]
    for c in range(got.shape[0] // 128):
        tile = got[c * 128 : c * 128 + 128].T
        conv_out[0, :, c * 128 : c * 128 + 128] = tile[0:64]
        conv_out[1, :, c * 128 : c * 128 + 128] = tile[64:128]

    for k in range(1, scens):
        env_copy(k).wait()
    best = envbuf[0]
    for k in range(1, scens):
        best = jnp.maximum(best, envbuf[k])
    env_out[...] = best


def shards(
    regions,
    scens,
    inverse_blocks,
    block_cols,
    source_current,
    node_decay,
    node_gain,
    voltage_init,
    branch_init,
    wave_init,
    line_node,
    line_delay,
    line_admittance,
    conv_region,
    conv_node,
    conv_power,
    conv_gains,
    conv_init,
    fault_node,
    fault_kind,
):
    scen_count, nodes = voltage_init.shape
    convs = conv_node.shape[0]
    slots = regions * ROWS
    tiles = nodes // 128
    vm = pl.BlockSpec(memory_space=pltpu.VMEM)
    wide = pltpu.VMEM((nodes, 128), F32)
    dma = pltpu.SemaphoreType.DMA
    volt, branch, wave, conv, env = pl.pallas_call(
        functools.partial(kernel, regions, scens),
        out_shape=(
            jax.ShapeDtypeStruct(voltage_init.shape, F32),
            jax.ShapeDtypeStruct(voltage_init.shape, F32),
            jax.ShapeDtypeStruct(wave_init.shape, F32),
            jax.ShapeDtypeStruct(conv_init.shape, F32),
            jax.ShapeDtypeStruct((tiles, 128), F32),
        ),
        in_specs=[pl.BlockSpec(memory_space=pl.ANY)]
        + [pl.BlockSpec(memory_space=pltpu.SMEM)] * 2
        + [vm] * 16,
        out_specs=(vm,) * 5,
        scratch_shapes=[
            pltpu.VMEM((regions, ROWS, 128), F32),
            pltpu.VMEM((convs, slots), BF16),
            pltpu.VMEM((NB, KB, BLK, BLK), F32),
            pltpu.VMEM((NB, 2 * BLK, 512), BF16),
            pltpu.VMEM((nodes, slots + 2 * LN), BF16),
            wide,
            wide,
            wide,
            wide,
            wide,
            wide,
            pltpu.VMEM((NB, BLK, 128), BF16),
            pltpu.VMEM((slots + 2 * LN, 128), BF16),
            pltpu.VMEM((slots, 128), F32),
            pltpu.VMEM((2 * LN, 128), F32),
            pltpu.VMEM((slots // 128, 128), jnp.int32),
            pltpu.SMEM((slots // 128, 128), jnp.int32),
            pltpu.VMEM((2 * LN, 128), F32),
            pltpu.VMEM((DMAX + STEPS, 2 * LN, 128), F32),
            pltpu.VMEM((regions, ROWS, 128), F32),
            pltpu.VMEM((regions, ROWS, 128), F32),
            pltpu.VMEM((slots, 128), F32),
            pltpu.VMEM((slots, 128), F32),
            pltpu.VMEM((slots, 128), F32),
            pltpu.VMEM((2 * LN, 128), F32),
            pltpu.VMEM((2 * LN, 128), F32),
            pltpu.VMEM((STEPS, 2, 64, 128), F32),
            pltpu.VMEM((STEPS, 2, 64, 128), F32),
            pltpu.VMEM((scens, tiles, 128), F32),
            dma,
            dma,
            dma((regions,)),
            dma((regions,)),
            dma,
            dma((regions,)),
            dma((regions,)),
            dma,
            dma((STEPS, 2)),
            dma((STEPS, 2)),
            dma((scens,)),
            dma((scens,)),
        ],
        compiler_params=pltpu.CompilerParams(
            collective_id=0, has_side_effects=True, vmem_limit_bytes=67043328
        ),
        name="transient",
    )(
        inverse_blocks,
        block_cols.T,
        line_node.reshape(2, LN),
        voltage_init,
        branch_init,
        wave_init,
        conv_init,
        node_decay.reshape(tiles, 128),
        node_gain.reshape(tiles, 128),
        source_current.reshape(tiles, 128),
        line_node.reshape(2, LN),
        line_delay.reshape(2, LN),
        line_admittance.reshape(2, LN),
        conv_region.T,
        conv_node.reshape(convs // 128, 128),
        conv_power.reshape(convs // 128, 128),
        conv_gains,
        fault_node.reshape(1, scen_count),
        fault_kind.reshape(1, scen_count),
    )
    return (volt, branch, wave, conv, env.reshape(nodes))


def solution(mesh):
    placed = (
        P("region", None, None, None),
        P("region", None),
        P("region"),
        P("region"),
        P("region"),
        P("scen", "region"),
        P("scen", "region"),
        P(None, "scen", "region"),
        P("region"),
        P("region"),
        P("region"),
        P("region", None),
        P("region"),
        P("region"),
        P(None, "region"),
        P(None, "scen", "region"),
        P("scen"),
        P("scen"),
    )
    return jax.shard_map(
        functools.partial(shards, mesh.shape["region"], mesh.shape["scen"]),
        mesh=mesh,
        in_specs=placed,
        out_specs=(
            P("scen", "region"),
            P("scen", "region"),
            P(None, "scen", "region"),
            P(None, "scen", "region"),
            P("region"),
        ),
        check_vma=False,
    )
```

```python
import functools

import jax
import jax.numpy as jnp
from jax import lax
from jax.experimental import pallas as pl
from jax.experimental.pallas import tpu as pltpu
from jax.sharding import PartitionSpec as P

STEPS = 4
BLK = 96
KB = 5
NB = 32
CAP = 14
ROWS = 16
LN = 128
DMAX = 8
NTILE = 1536
GROUP = 16
MESH = pl.DeviceIdType.MESH
F32 = jnp.float32
BF16 = jnp.bfloat16


def lanes(shape, axis):
    return lax.broadcasted_iota(jnp.int32, shape, axis)


def low_half(shape):
    return lanes(shape, len(shape) - 1) % 128 < 64


def both(z):
    return z + pltpu.roll(z, 64, 1)


def split(x):
    lead = x.astype(BF16).astype(F32)
    return jnp.where(low_half(x.shape), lead, x - lead).astype(BF16)


def column(row):
    return jnp.broadcast_to(row, (128, 128)).T


def kernel(
    regions,
    scens,
    blocks_ref,
    cols_ref,
    ends_ref,
    vinit_ref,
    binit_ref,
    winit_ref,
    cinit_ref,
    decay_ref,
    gain_ref,
    source_ref,
    lnode_ref,
    ldelay_ref,
    ladm_ref,
    region_ref,
    cnode_ref,
    cpower_ref,
    cgains_ref,
    fnode_ref,
    fkind_ref,
    volt_out,
    branch_out,
    wave_out,
    conv_out,
    env_out,
    payload_ref,
    back_ref,
    wraw,
    wmat,
    scat,
    volt,
    branch,
    env,
    decay,
    gain,
    source,
    xop,
    aop,
    measured,
    ends,
    indexv,
    index,
    drive,
    hist,
    state,
    ret,
    power,
    gamps,
    gfilt,
    ldelay,
    ladm,
    sendbuf,
    arrived,
    envbuf,
    load_sem,
    index_sem,
    fsend,
    frecv,
    fself,
    bsend,
    brecv,
    bself,
    lsend,
    lrecv,
    esend,
    erecv,
):
    me = lax.axis_index("region")
    sc = lax.axis_index("scen")
    nxt = lax.rem(me + 1, regions)
    prv = lax.rem(me + regions - 1, regions)
    slots = regions * ROWS
    nodes = volt.shape[0]
    ctile = min(256, slots)
    pairs = 128 // ROWS

    state[:, CAP + 1 :, :] = jnp.zeros((regions, ROWS - CAP - 1, 128), F32)
    ret[:, CAP:, :] = jnp.zeros((regions, ROWS - CAP, 128), F32)

    barrier = pltpu.get_barrier_semaphore()

    def greet(k, _):
        pl.semaphore_signal(
            barrier, inc=1, device_id={"region": lax.rem(me + k, regions)}, device_id_type=MESH
        )
        return 0

    lax.fori_loop(1, regions, greet, 0)
    for k in range(1, scens):
        pl.semaphore_signal(
            barrier, inc=1, device_id={"scen": lax.rem(sc + k, scens)}, device_id_type=MESH
        )
    load = pltpu.make_async_copy(blocks_ref, wraw, load_sem)
    load.start()

    convs = back_ref.shape[0]
    lane = lanes((convs, 128), 1)
    target = jnp.concatenate(
        [column(region_ref[:, h * 128 : h * 128 + 128].astype(F32)) for h in range(convs // 128)], axis=0
    )
    member = jnp.where(target == lane.astype(F32), 1.0, 0.0)
    before = jnp.where(lanes((convs, convs), 0) > lanes((convs, convs), 1), 1.0, 0.0)
    earlier = jnp.dot(before.astype(BF16), member.astype(BF16), preferred_element_type=F32)
    rank = jnp.sum(earlier * member, axis=1, keepdims=True)
    position = target * float(ROWS) + rank
    for c in range(slots // 128):
        back_ref[:, c * 128 : c * 128 + 128] = jnp.where(
            position == (lane + c * 128).astype(F32), 1.0, 0.0
        ).astype(BF16)
    content = jnp.concatenate([cinit_ref[0], cinit_ref[1]], axis=0)
    lead = content.astype(BF16)
    rest = (content - lead.astype(F32)).astype(BF16)
    content = jnp.dot(
        jnp.concatenate([lead, rest], axis=0), back_ref[...], preferred_element_type=F32
    )
    content = content[0:128] + content[128:256]
    for c in range(slots // 128):
        payload_ref[c * pairs : c * pairs + pairs] = content[:, c * 128 : c * 128 + 128].T.reshape(
            pairs, ROWS, 128
        )
    params = jnp.concatenate(
        [
            jnp.concatenate(
                [
                    cnode_ref[h : h + 1, :].astype(F32) + 1.0,
                    cpower_ref[h : h + 1, :],
                    cgains_ref[:, h * 128 : h * 128 + 128],
                    jnp.zeros((124, 128), F32),
                ],
                axis=0,
            ).T
            for h in range(convs // 128)
        ],
        axis=0,
    )
    values = jnp.zeros((convs, 128), F32)
    for w in range(4):
        values = values + jnp.where(lane // ROWS == w, params[:, w : w + 1], 0.0)
    values = jnp.where((lane % ROWS).astype(F32) == rank, values, 0.0)
    lead = values.astype(BF16).astype(F32)
    values = jnp.where(lane < 64, lead, pltpu.roll(values - lead, 64, 1)).astype(BF16)
    owners = jnp.concatenate(
        [member[h * 128 : h * 128 + 128].T for h in range(convs // 128)], axis=1
    ).astype(BF16)
    payload_ref[:, CAP, :] = both(jnp.dot(owners, values, preferred_element_type=F32))[0:regions]

    pl.semaphore_wait(barrier, regions - 1 + scens - 1)

    def forward(peer):
        return pltpu.make_async_remote_copy(
            src_ref=payload_ref.at[peer, 0 : CAP + 1],
            dst_ref=state.at[me, 0 : CAP + 1],
            send_sem=fsend.at[peer],
            recv_sem=frecv.at[me],
            device_id={"region": peer},
            device_id_type=MESH,
        )

    def backward(peer):
        return pltpu.make_async_remote_copy(
            src_ref=state.at[peer, 0:CAP],
            dst_ref=ret.at[me, 0:CAP],
            send_sem=bsend.at[peer],
            recv_sem=brecv.at[me],
            device_id={"region": peer},
            device_id_type=MESH,
        )

    half = regions // 2
    forward(lax.rem(me + half, regions)).start()

    def start_forward(k, _):
        forward(lax.rem(me + half - k, regions)).start()
        forward(lax.rem(me + half + k, regions)).start()
        return 0

    lax.fori_loop(1, half, start_forward, 0)
    own = pltpu.make_async_copy(
        payload_ref.at[me, 0 : CAP + 1], state.at[me, 0 : CAP + 1], fself
    )
    own.start()

    def place(i, _):
        for q in range(2):
            c = 2 * i + q
            at = pl.ds(pl.multiple_of(c * 128, 128), 128)
            v = vinit_ref[:, at]
            volt[at, :] = jnp.concatenate([v, v], axis=0).T
            b = binit_ref[:, at]
            branch[at, :] = jnp.concatenate([b, b], axis=0).T
            decay[at, :] = column(decay_ref[pl.ds(c, 1), :])
            gain[at, :] = column(gain_ref[pl.ds(c, 1), :])
            source[at, :] = column(source_ref[pl.ds(c, 1), :])
            env[at, :] = jnp.zeros((128, 128), F32)
        return 0

    lax.fori_loop(0, nodes // 256, place, 0)

    def place_wave(d, _):
        for h in range(2):
            w = winit_ref[d, :, h * 128 : h * 128 + 128]
            hist[DMAX - 1 - d, h * 128 : h * 128 + 128, :] = jnp.concatenate([w, w], axis=0).T
        return 0

    lax.fori_loop(0, DMAX, place_wave, 0)

    for h in range(2):
        at = slice(h * 128, h * 128 + 128)
        ldelay[at, :] = column(ldelay_ref[h : h + 1, :].astype(F32))
        ladm[at, :] = 2.0 * column(ladm_ref[h : h + 1, :])
        def line_scatter(c, _):
            here = (lanes((128, 128), 0) + c * 128).astype(F32)
            row = lnode_ref[h : h + 1, :].astype(F32)
            scat[pl.ds(pl.multiple_of(c * 128, 128), 128), slots + h * 128 : slots + h * 128 + 128] = (
                jnp.where(row == here, 1.0, 0.0).astype(BF16)
            )
            return 0

        lax.fori_loop(0, nodes // 128, line_scatter, 0)

    load.wait()

    def prepare(b, _):
        parts = [wraw[b, k] for k in range(KB)]
        whole = jnp.concatenate(parts + [jnp.zeros((BLK, 512 - KB * BLK), F32)], axis=1)
        lead = whole.astype(BF16)
        wmat[b, 0:BLK, :] = lead
        wmat[b, BLK : 2 * BLK, :] = (whole - lead.astype(F32)).astype(BF16)
        return 0

    lax.fori_loop(0, NB, prepare, 0)

    own.wait()

    def wait_forward(k, _):
        forward(lax.rem(me + k, regions)).wait_send()
        return 0

    lax.fori_loop(1, regions, wait_forward, 0)

    def arrive_forward(k, _):
        frm = lax.rem(me + regions - k, regions)
        pltpu.make_async_remote_copy(
            src_ref=payload_ref.at[frm, 0 : CAP + 1],
            dst_ref=state.at[frm, 0 : CAP + 1],
            send_sem=fsend.at[frm],
            recv_sem=frecv.at[frm],
            device_id={"region": frm},
            device_id_type=MESH,
        ).wait_recv()
        return 0

    lax.fori_loop(1, regions, arrive_forward, 0)

    params = state[:, CAP, :]
    lead = params.astype(BF16).astype(F32)
    lane64 = lanes((regions, 128), 1) < 64
    pair = jnp.where(lane64, lead, pltpu.roll(params - lead, 64, 1))
    fold = (lanes((128, slots), 0) % 64 == lanes((128, slots), 1) % ROWS).astype(F32).astype(BF16)
    spread = jnp.dot(pair.astype(BF16), fold, preferred_element_type=F32)
    mine = lanes((regions, slots), 0) == lanes((regions, slots), 1) // ROWS
    noderow = jnp.sum(jnp.where(mine, spread, 0.0), axis=0, keepdims=True)

    for r in range(slots // 128):
        number = noderow[:, r * 128 : r * 128 + 128].astype(jnp.int32) - 1
        indexv[r : r + 1, :] = jnp.clip(number, 0, nodes - 1)
    to_scalars = pltpu.make_async_copy(indexv, index, index_sem)
    to_scalars.start()

    def conv_scatter(c, _):
        here = (lanes((128, slots), 0) + (c * 128 + 1)).astype(F32)
        scat[pl.ds(pl.multiple_of(c * 128, 128), 128), 0:slots] = (
            jnp.where(noderow == here, 1.0, 0.0).astype(BF16)
        )
        return 0

    lax.fori_loop(0, nodes // 128, conv_scatter, 0)

    pick = ((lanes((128, 384), 0) % 64) // ROWS == lanes((128, 384), 1) // 128 + 1).astype(F32).astype(BF16)

    def conv_param(i, _):
        r0 = i * (ctile // ROWS)
        prm = state[pl.ds(r0, ctile // ROWS), CAP, :]
        ld = prm.astype(BF16).astype(F32)
        both_parts = jnp.where(low_half(prm.shape), ld, pltpu.roll(prm - ld, 64, 1))
        rep = jnp.broadcast_to(both_parts[:, None, :], (ctile // ROWS, ROWS, 128)).reshape(ctile, 128)
        slot = lanes((ctile, 128), 0) % ROWS
        rep = jnp.where(lanes((ctile, 128), 1) % ROWS == slot, rep, 0.0).astype(BF16)
        got = jnp.dot(rep, pick, preferred_element_type=F32)
        at = pl.ds(pl.multiple_of(i * ctile, ctile), ctile)
        power[at, :] = got[:, 0:128]
        gamps[at, :] = got[:, 128:256]
        gfilt[at, :] = got[:, 256:384]
        return 0

    lax.fori_loop(0, slots // ctile, conv_param, 0)

    measured[...] = jnp.zeros_like(measured)
    to_scalars.wait()
    fault = (fnode_ref[...] - me * nodes).astype(F32)
    fault = jnp.concatenate([fault, fault], axis=1)
    conduct = 0.25 * jnp.left_shift(1, fkind_ref[...]).astype(F32)
    conduct = jnp.concatenate([conduct, conduct], axis=1)

    def line_copies(t):
        return [
            pltpu.make_async_remote_copy(
                src_ref=sendbuf.at[t, side],
                dst_ref=arrived.at[t, side],
                send_sem=lsend.at[t, side],
                recv_sem=lrecv.at[t, side],
                device_id={"region": to},
                device_id_type=MESH,
            )
            for side, to in ((0, nxt), (1, prv))
        ]

    def take_arrivals(t):
        for side, copy in enumerate(line_copies(t)):
            copy.wait()
            p = arrived[t, side]
            q = pltpu.roll(p, 64, 1)
            low = low_half(p.shape)
            hist[DMAX + t, side * LN : side * LN + 64, :] = jnp.where(low, p, q)
            hist[DMAX + t, side * LN + 64 : side * LN + 128, :] = jnp.where(low, q, p)

    def step(t, last):
        def conv(i, _):
            for q in range(pairs):
                for j in range(CAP):
                    measured[pl.ds(i * 128 + q * ROWS + j, 1), :] = volt[jnp.clip(index[i, q * ROWS + j], 0, nodes - 1)][None]
            at = pl.ds(pl.multiple_of(i * 128, 128), 128)
            m = measured[at, :]
            rows = pl.ds(i * pairs, pairs)
            f = state[rows].reshape(128, 128)
            low = low_half(f.shape)
            filt = f + gfilt[at, :] * (m - f)
            full = jnp.where(low, filt, pltpu.roll(filt, 64, 1))
            goal = power[at, :] * full / (1.0 + full * full)
            amps = f + gamps[at, :] * (goal - f)
            state[rows] = jnp.where(low, filt, amps).reshape(pairs, ROWS, 128)
            aop[at, :] = split(jnp.where(low, pltpu.roll(amps, 64, 1), amps))
            return 0

        lax.fori_loop(0, slots // 128, conv, 0)

        if last:

            backward(lax.rem(me + half, regions)).start()

            def start_backward(k, _):
                backward(lax.rem(me + half - k, regions)).start()
                backward(lax.rem(me + half + k, regions)).start()
                return 0

            lax.fori_loop(1, half, start_backward, 0)
            pltpu.make_async_copy(state.at[me, 0:CAP], ret.at[me, 0:CAP], bself).start()

        if t > 0:
            take_arrivals(t - 1)
        d = jnp.zeros((2 * LN, 128), F32)
        for k in range(1, DMAX + 1):
            d = d + jnp.where(ldelay[...] == float(k), hist[DMAX + t - k], 0.0)
        drive[...] = d
        aop[slots : slots + 2 * LN, :] = split(d)

        def assemble(i, _):
            at = pl.ds(pl.multiple_of(i * NTILE, NTILE), NTILE)
            z = both(jnp.dot(scat[at, :], aop[...], preferred_element_type=F32))
            v = volt[at, :]
            b = decay[at, :] * branch[at, :] + gain[at, :] * v
            branch[at, :] = b
            here = (lanes((NTILE, 128), 0) + i * NTILE).astype(F32)
            hit = jnp.where(fault == here, conduct * v, 0.0)
            x = split(source[at, :] - b - hit + z)
            for q in range(NTILE // BLK):
                xop[NTILE // BLK * i + q] = x[q * BLK : (q + 1) * BLK]
            return 0

        lax.fori_loop(0, nodes // NTILE, assemble, 0)

        def solve(i, _):
            found = []
            for q in range(GROUP):
                b = i * GROUP + q
                parts = [xop[cols_ref[k, b]] for k in range(KB)]
                x = jnp.concatenate(parts + [jnp.zeros((512 - KB * BLK, 128), BF16)], axis=0)
                z = jnp.dot(wmat[b], x, preferred_element_type=F32)
                found.append(both(z[0:BLK] + z[BLK : 2 * BLK]))
            at = pl.ds(pl.multiple_of(i * (GROUP * BLK), GROUP * BLK), GROUP * BLK)
            v = jnp.concatenate(found, axis=0)
            volt[at, :] = v
            env[at, :] = jnp.maximum(env[at, :], jnp.abs(v))
            return 0

        lax.fori_loop(0, NB // GROUP, solve, 0)

        def take_ends(i, _):
            for j in range(LN):
                ends[pl.ds(i * LN + j, 1), :] = volt[ends_ref[i, j]][None]
            return 0

        lax.fori_loop(0, 2, take_ends, 0)
        launch = ladm[...] * ends[...] - drive[...]
        low = low_half((64, 128))
        sendbuf[t, 0] = jnp.where(low, launch[LN : LN + 64], launch[LN + 64 : 2 * LN])
        sendbuf[t, 1] = jnp.where(low, launch[0:64], launch[64:LN])
        for copy in line_copies(t):
            copy.start()

    for t in range(STEPS):
        step(t, t == STEPS - 1)

    def peak(i, _):
        rows = []
        for q in range(8):
            at = pl.ds(pl.multiple_of((8 * i + q) * 128, 128), 128)
            rows.append(jnp.max(env[at, :].T, axis=0, keepdims=True))
        envbuf[sc, pl.ds(pl.multiple_of(8 * i, 8), 8), :] = jnp.concatenate(rows, axis=0)
        return 0

    lax.fori_loop(0, nodes // 1024, peak, 0)

    def env_copy(k):
        return pltpu.make_async_remote_copy(
            src_ref=envbuf.at[sc],
            dst_ref=envbuf.at[sc],
            send_sem=esend.at[k],
            recv_sem=erecv.at[k],
            device_id={"scen": lax.rem(sc + k, scens)},
            device_id_type=MESH,
        )

    for k in range(1, scens):
        env_copy(k).start()

    def finish(i, _):
        for q in range(4):
            at = pl.ds(pl.multiple_of((4 * i + q) * 128, 128), 128)
            volt_out[:, at] = volt[at, :].T[0:64]
            branch_out[:, at] = branch[at, :].T[0:64]
        return 0

    lax.fori_loop(0, nodes // 512, finish, 0)

    take_arrivals(STEPS - 1)
    for j in range(STEPS):
        for h in range(2):
            at = slice(h * 128, h * 128 + 128)
            wave_out[j, :, at] = hist[DMAX + STEPS - 1 - j, at, :].T[0:64]
    for j in range(STEPS, DMAX):
        wave_out[j] = winit_ref[j - STEPS]

    pltpu.make_async_copy(state.at[me, 0:CAP], ret.at[me, 0:CAP], bself).wait()

    def wait_backward(k, _):
        backward(lax.rem(me + k, regions)).wait_send()
        return 0

    lax.fori_loop(1, regions, wait_backward, 0)

    def arrive_backward(k, _):
        frm = lax.rem(me + regions - k, regions)
        pltpu.make_async_remote_copy(
            src_ref=state.at[frm, 0:CAP],
            dst_ref=ret.at[frm, 0:CAP],
            send_sem=bsend.at[frm],
            recv_sem=brecv.at[frm],
            device_id={"region": frm},
            device_id_type=MESH,
        ).wait_recv()
        return 0

    lax.fori_loop(1, regions, arrive_backward, 0)

    r = ret[...].reshape(slots, 128)
    lead = r.astype(BF16)
    rest = (r - lead.astype(F32)).astype(BF16)
    got = jnp.dot(back_ref[...], jnp.concatenate([lead, rest], axis=1), preferred_element_type=F32)
    got = got[:, 0:128] + got[:, 128:256]
    for c in range(got.shape[0] // 128):
        tile = got[c * 128 : c * 128 + 128].T
        conv_out[0, :, c * 128 : c * 128 + 128] = tile[0:64]
        conv_out[1, :, c * 128 : c * 128 + 128] = tile[64:128]

    for k in range(1, scens):
        env_copy(k).wait()
    best = envbuf[0]
    for k in range(1, scens):
        best = jnp.maximum(best, envbuf[k])
    env_out[...] = best


def deliver(*refs):
    count = len(refs[:-2]) // 3
    taken, given, held = refs[:count], refs[count : 2 * count], refs[2 * count : 3 * count]
    in_sem, out_sem = refs[-2:]
    ins = [pltpu.make_async_copy(taken[i], held[i], in_sem.at[i]) for i in range(count)]
    outs = [pltpu.make_async_copy(held[i], given[i], out_sem.at[i]) for i in range(count)]
    for copy in ins:
        copy.start()
    for copy, then in zip(ins, outs):
        copy.wait()
        then.start()
    for copy in outs:
        copy.wait()


def shards(
    regions,
    scens,
    inverse_blocks,
    block_cols,
    source_current,
    node_decay,
    node_gain,
    voltage_init,
    branch_init,
    wave_init,
    line_node,
    line_delay,
    line_admittance,
    conv_region,
    conv_node,
    conv_power,
    conv_gains,
    conv_init,
    fault_node,
    fault_kind,
):
    scen_count, nodes = voltage_init.shape
    convs = conv_node.shape[0]
    slots = regions * ROWS
    tiles = nodes // 128
    vm = pl.BlockSpec(memory_space=pltpu.VMEM)
    wide = pltpu.VMEM((nodes, 128), F32)
    dma = pltpu.SemaphoreType.DMA
    results = pl.pallas_call(
        functools.partial(kernel, regions, scens),
        out_shape=(
            jax.ShapeDtypeStruct(voltage_init.shape, F32),
            jax.ShapeDtypeStruct(voltage_init.shape, F32),
            jax.ShapeDtypeStruct(wave_init.shape, F32),
            jax.ShapeDtypeStruct(conv_init.shape, F32),
            jax.ShapeDtypeStruct((tiles, 128), F32),
        ),
        in_specs=[pl.BlockSpec(memory_space=pl.ANY)]
        + [pl.BlockSpec(memory_space=pltpu.SMEM)] * 2
        + [vm] * 16,
        out_specs=(vm,) * 5,
        scratch_shapes=[
            pltpu.VMEM((regions, ROWS, 128), F32),
            pltpu.VMEM((convs, slots), BF16),
            pltpu.VMEM((NB, KB, BLK, BLK), F32),
            pltpu.VMEM((NB, 2 * BLK, 512), BF16),
            pltpu.VMEM((nodes, slots + 2 * LN), BF16),
            wide,
            wide,
            wide,
            wide,
            wide,
            wide,
            pltpu.VMEM((NB, BLK, 128), BF16),
            pltpu.VMEM((slots + 2 * LN, 128), BF16),
            pltpu.VMEM((slots, 128), F32),
            pltpu.VMEM((2 * LN, 128), F32),
            pltpu.VMEM((slots // 128, 128), jnp.int32),
            pltpu.SMEM((slots // 128, 128), jnp.int32),
            pltpu.VMEM((2 * LN, 128), F32),
            pltpu.VMEM((DMAX + STEPS, 2 * LN, 128), F32),
            pltpu.VMEM((regions, ROWS, 128), F32),
            pltpu.VMEM((regions, ROWS, 128), F32),
            pltpu.VMEM((slots, 128), F32),
            pltpu.VMEM((slots, 128), F32),
            pltpu.VMEM((slots, 128), F32),
            pltpu.VMEM((2 * LN, 128), F32),
            pltpu.VMEM((2 * LN, 128), F32),
            pltpu.VMEM((STEPS, 2, 64, 128), F32),
            pltpu.VMEM((STEPS, 2, 64, 128), F32),
            pltpu.VMEM((scens, tiles, 128), F32),
            dma,
            dma,
            dma((regions,)),
            dma((regions,)),
            dma,
            dma((regions,)),
            dma((regions,)),
            dma,
            dma((STEPS, 2)),
            dma((STEPS, 2)),
            dma((scens,)),
            dma((scens,)),
        ],
        compiler_params=pltpu.CompilerParams(
            collective_id=0, has_side_effects=True, vmem_limit_bytes=67043328
        ),
        name="transient",
    )(
        inverse_blocks,
        block_cols.T,
        line_node.reshape(2, LN),
        voltage_init,
        branch_init,
        wave_init,
        conv_init,
        node_decay.reshape(tiles, 128),
        node_gain.reshape(tiles, 128),
        source_current.reshape(tiles, 128),
        line_node.reshape(2, LN),
        line_delay.reshape(2, LN),
        line_admittance.reshape(2, LN),
        conv_region.T,
        conv_node.reshape(convs // 128, 128),
        conv_power.reshape(convs // 128, 128),
        conv_gains,
        fault_node.reshape(1, scen_count),
        fault_kind.reshape(1, scen_count),
    )
    shapes = [jax.ShapeDtypeStruct(r.shape, r.dtype) for r in results]
    volt, branch, wave, conv, env = pl.pallas_call(
        deliver,
        out_shape=tuple(shapes),
        in_specs=[pl.BlockSpec(memory_space=pl.ANY)] * len(shapes),
        out_specs=(pl.BlockSpec(memory_space=pl.ANY),) * len(shapes),
        scratch_shapes=[pltpu.VMEM(r.shape, r.dtype) for r in shapes] + [dma((len(shapes),))] * 2,
        compiler_params=pltpu.CompilerParams(vmem_limit_bytes=67043328),
        name="deliver",
    )(*results)
    return (volt, branch, wave, conv, env.reshape(nodes))


def solution(mesh):
    placed = (
        P("region", None, None, None),
        P("region", None),
        P("region"),
        P("region"),
        P("region"),
        P("scen", "region"),
        P("scen", "region"),
        P(None, "scen", "region"),
        P("region"),
        P("region"),
        P("region"),
        P("region", None),
        P("region"),
        P("region"),
        P(None, "region"),
        P(None, "scen", "region"),
        P("scen"),
        P("scen"),
    )
    return jax.shard_map(
        functools.partial(shards, mesh.shape["region"], mesh.shape["scen"]),
        mesh=mesh,
        in_specs=placed,
        out_specs=(
            P("scen", "region"),
            P("scen", "region"),
            P(None, "scen", "region"),
            P(None, "scen", "region"),
            P("region"),
        ),
        check_vma=False,
    )
```

```python
import functools

import jax
import jax.numpy as jnp
from jax import lax
from jax.experimental import pallas as pl
from jax.experimental.pallas import tpu as pltpu
from jax.sharding import PartitionSpec as P

STEPS = 4
BLK = 96
KB = 5
NB = 32
CAP = 14
ROWS = 16
LN = 128
DMAX = 8
NTILE = 1536
GROUP = 16
MESH = pl.DeviceIdType.MESH
F32 = jnp.float32
BF16 = jnp.bfloat16


def lanes(shape, axis):
    return lax.broadcasted_iota(jnp.int32, shape, axis)


def low_half(shape):
    return lanes(shape, len(shape) - 1) % 128 < 64


def both(z):
    return z + pltpu.roll(z, 64, 1)


def split(x):
    lead = x.astype(BF16).astype(F32)
    return jnp.where(low_half(x.shape), lead, x - lead).astype(BF16)


def column(row):
    return jnp.broadcast_to(row, (128, 128)).T


def kernel(
    regions,
    scens,
    blocks_ref,
    cols_ref,
    ends_ref,
    vinit_ref,
    binit_ref,
    winit_ref,
    cinit_ref,
    decay_ref,
    gain_ref,
    source_ref,
    lnode_ref,
    ldelay_ref,
    ladm_ref,
    region_ref,
    cnode_ref,
    cpower_ref,
    cgains_ref,
    fnode_ref,
    fkind_ref,
    volt_out,
    branch_out,
    wave_out,
    conv_out,
    env_out,
    payload_ref,
    params_ref,
    back_ref,
    wraw,
    wmat,
    scat,
    volt,
    branch,
    env,
    decay,
    gain,
    source,
    xop,
    aop,
    measured,
    ends,
    indexv,
    index,
    drive,
    hist,
    state,
    ret,
    power,
    gamps,
    gfilt,
    ldelay,
    ladm,
    sendbuf,
    arrived,
    envbuf,
    load_sem,
    index_sem,
    psend,
    precv,
    pself,
    fsend,
    frecv,
    fself,
    bsend,
    brecv,
    bself,
    lsend,
    lrecv,
    esend,
    erecv,
):
    me = lax.axis_index("region")
    sc = lax.axis_index("scen")
    nxt = lax.rem(me + 1, regions)
    prv = lax.rem(me + regions - 1, regions)
    slots = regions * ROWS
    nodes = volt.shape[0]
    ctile = min(256, slots)
    pairs = 128 // ROWS

    state[:, CAP:, :] = jnp.zeros((regions, ROWS - CAP, 128), F32)
    ret[:, CAP:, :] = jnp.zeros((regions, ROWS - CAP, 128), F32)

    barrier = pltpu.get_barrier_semaphore()

    def greet(k, _):
        pl.semaphore_signal(
            barrier, inc=1, device_id={"region": lax.rem(me + k, regions)}, device_id_type=MESH
        )
        return 0

    lax.fori_loop(1, regions, greet, 0)
    for k in range(1, scens):
        pl.semaphore_signal(
            barrier, inc=1, device_id={"scen": lax.rem(sc + k, scens)}, device_id_type=MESH
        )
    load = pltpu.make_async_copy(blocks_ref, wraw, load_sem)
    load.start()

    convs = back_ref.shape[0]
    lane = lanes((convs, 128), 1)
    target = jnp.concatenate(
        [column(region_ref[:, h * 128 : h * 128 + 128].astype(F32)) for h in range(convs // 128)], axis=0
    )
    member = jnp.where(target == lane.astype(F32), 1.0, 0.0)
    before = jnp.where(lanes((convs, convs), 0) > lanes((convs, convs), 1), 1.0, 0.0)
    earlier = jnp.dot(before.astype(BF16), member.astype(BF16), preferred_element_type=F32)
    rank = jnp.sum(earlier * member, axis=1, keepdims=True)
    position = target * float(ROWS) + rank
    for c in range(slots // 128):
        back_ref[:, c * 128 : c * 128 + 128] = jnp.where(
            position == (lane + c * 128).astype(F32), 1.0, 0.0
        ).astype(BF16)
    content = jnp.concatenate([cinit_ref[0], cinit_ref[1]], axis=0)
    lead = content.astype(BF16)
    rest = (content - lead.astype(F32)).astype(BF16)
    content = jnp.dot(
        jnp.concatenate([lead, rest], axis=0), back_ref[...], preferred_element_type=F32
    )
    content = content[0:128] + content[128:256]
    for c in range(slots // 128):
        payload_ref[c * pairs : c * pairs + pairs] = content[:, c * 128 : c * 128 + 128].T.reshape(
            pairs, ROWS, 128
        )
    params = jnp.concatenate(
        [
            jnp.concatenate(
                [
                    cnode_ref[h : h + 1, :].astype(F32) + 1.0,
                    cpower_ref[h : h + 1, :],
                    cgains_ref[:, h * 128 : h * 128 + 128],
                    jnp.zeros((124, 128), F32),
                ],
                axis=0,
            ).T
            for h in range(convs // 128)
        ],
        axis=0,
    )
    values = jnp.zeros((convs, 128), F32)
    for w in range(4):
        values = values + jnp.where(lane // ROWS == w, params[:, w : w + 1], 0.0)
    values = jnp.where((lane % ROWS).astype(F32) == rank, values, 0.0)
    lead = values.astype(BF16).astype(F32)
    values = jnp.where(lane < 64, lead, pltpu.roll(values - lead, 64, 1)).astype(BF16)
    owners = jnp.concatenate(
        [member[h * 128 : h * 128 + 128].T for h in range(convs // 128)], axis=1
    ).astype(BF16)
    payload_ref[:, CAP, :] = both(jnp.dot(owners, values, preferred_element_type=F32))[0:regions]

    pl.semaphore_wait(barrier, regions - 1 + scens - 1)

    def forward(peer):
        return pltpu.make_async_remote_copy(
            src_ref=payload_ref.at[peer, 0:CAP],
            dst_ref=state.at[me, 0:CAP],
            send_sem=fsend.at[peer],
            recv_sem=frecv.at[me],
            device_id={"region": peer},
            device_id_type=MESH,
        )

    def announce(peer):
        return pltpu.make_async_remote_copy(
            src_ref=payload_ref.at[peer, CAP],
            dst_ref=params_ref.at[me],
            send_sem=psend.at[peer],
            recv_sem=precv.at[me],
            device_id={"region": peer},
            device_id_type=MESH,
        )

    def backward(peer):
        return pltpu.make_async_remote_copy(
            src_ref=state.at[peer, 0:CAP],
            dst_ref=ret.at[me, 0:CAP],
            send_sem=bsend.at[peer],
            recv_sem=brecv.at[me],
            device_id={"region": peer},
            device_id_type=MESH,
        )

    half = regions // 2
    announce(lax.rem(me + half, regions)).start()

    def start_announce(k, _):
        announce(lax.rem(me + half - k, regions)).start()
        announce(lax.rem(me + half + k, regions)).start()
        return 0

    lax.fori_loop(1, half, start_announce, 0)
    own_params = pltpu.make_async_copy(payload_ref.at[me, CAP], params_ref.at[me], pself)
    own_params.start()
    forward(lax.rem(me + half, regions)).start()

    def start_forward(k, _):
        forward(lax.rem(me + half - k, regions)).start()
        forward(lax.rem(me + half + k, regions)).start()
        return 0

    lax.fori_loop(1, half, start_forward, 0)
    own = pltpu.make_async_copy(payload_ref.at[me, 0:CAP], state.at[me, 0:CAP], fself)
    own.start()

    def place(i, _):
        for q in range(2):
            c = 2 * i + q
            at = pl.ds(pl.multiple_of(c * 128, 128), 128)
            v = vinit_ref[:, at]
            volt[at, :] = jnp.concatenate([v, v], axis=0).T
            b = binit_ref[:, at]
            branch[at, :] = jnp.concatenate([b, b], axis=0).T
            decay[at, :] = column(decay_ref[pl.ds(c, 1), :])
            gain[at, :] = column(gain_ref[pl.ds(c, 1), :])
            source[at, :] = column(source_ref[pl.ds(c, 1), :])
            env[at, :] = jnp.zeros((128, 128), F32)
        return 0

    lax.fori_loop(0, nodes // 256, place, 0)

    def place_wave(d, _):
        for h in range(2):
            w = winit_ref[d, :, h * 128 : h * 128 + 128]
            hist[DMAX - 1 - d, h * 128 : h * 128 + 128, :] = jnp.concatenate([w, w], axis=0).T
        return 0

    lax.fori_loop(0, DMAX, place_wave, 0)

    for h in range(2):
        at = slice(h * 128, h * 128 + 128)
        ldelay[at, :] = column(ldelay_ref[h : h + 1, :].astype(F32))
        ladm[at, :] = 2.0 * column(ladm_ref[h : h + 1, :])
        def line_scatter(c, _):
            here = (lanes((128, 128), 0) + c * 128).astype(F32)
            row = lnode_ref[h : h + 1, :].astype(F32)
            scat[pl.ds(pl.multiple_of(c * 128, 128), 128), slots + h * 128 : slots + h * 128 + 128] = (
                jnp.where(row == here, 1.0, 0.0).astype(BF16)
            )
            return 0

        lax.fori_loop(0, nodes // 128, line_scatter, 0)

    load.wait()

    def prepare(b, _):
        parts = [wraw[b, k] for k in range(KB)]
        whole = jnp.concatenate(parts + [jnp.zeros((BLK, 512 - KB * BLK), F32)], axis=1)
        lead = whole.astype(BF16)
        wmat[b, 0:BLK, :] = lead
        wmat[b, BLK : 2 * BLK, :] = (whole - lead.astype(F32)).astype(BF16)
        return 0

    lax.fori_loop(0, NB, prepare, 0)

    own_params.wait()

    def wait_announce(k, _):
        announce(lax.rem(me + k, regions)).wait_send()
        return 0

    lax.fori_loop(1, regions, wait_announce, 0)

    def arrive_announce(k, _):
        frm = lax.rem(me + regions - k, regions)
        pltpu.make_async_remote_copy(
            src_ref=payload_ref.at[frm, CAP],
            dst_ref=params_ref.at[frm],
            send_sem=psend.at[frm],
            recv_sem=precv.at[frm],
            device_id={"region": frm},
            device_id_type=MESH,
        ).wait_recv()
        return 0

    lax.fori_loop(1, regions, arrive_announce, 0)

    params = params_ref[...]
    lead = params.astype(BF16).astype(F32)
    lane64 = lanes((regions, 128), 1) < 64
    pair = jnp.where(lane64, lead, pltpu.roll(params - lead, 64, 1))
    fold = (lanes((128, slots), 0) % 64 == lanes((128, slots), 1) % ROWS).astype(F32).astype(BF16)
    spread = jnp.dot(pair.astype(BF16), fold, preferred_element_type=F32)
    mine = lanes((regions, slots), 0) == lanes((regions, slots), 1) // ROWS
    noderow = jnp.sum(jnp.where(mine, spread, 0.0), axis=0, keepdims=True)

    for r in range(slots // 128):
        number = noderow[:, r * 128 : r * 128 + 128].astype(jnp.int32) - 1
        indexv[r : r + 1, :] = jnp.clip(number, 0, nodes - 1)
    to_scalars = pltpu.make_async_copy(indexv, index, index_sem)
    to_scalars.start()

    def conv_scatter(c, _):
        here = (lanes((128, slots), 0) + (c * 128 + 1)).astype(F32)
        scat[pl.ds(pl.multiple_of(c * 128, 128), 128), 0:slots] = (
            jnp.where(noderow == here, 1.0, 0.0).astype(BF16)
        )
        return 0

    lax.fori_loop(0, nodes // 128, conv_scatter, 0)

    pick = ((lanes((128, 384), 0) % 64) // ROWS == lanes((128, 384), 1) // 128 + 1).astype(F32).astype(BF16)

    def conv_param(i, _):
        r0 = i * (ctile // ROWS)
        prm = params_ref[pl.ds(r0, ctile // ROWS), :]
        ld = prm.astype(BF16).astype(F32)
        both_parts = jnp.where(low_half(prm.shape), ld, pltpu.roll(prm - ld, 64, 1))
        rep = jnp.broadcast_to(both_parts[:, None, :], (ctile // ROWS, ROWS, 128)).reshape(ctile, 128)
        slot = lanes((ctile, 128), 0) % ROWS
        rep = jnp.where(lanes((ctile, 128), 1) % ROWS == slot, rep, 0.0).astype(BF16)
        got = jnp.dot(rep, pick, preferred_element_type=F32)
        at = pl.ds(pl.multiple_of(i * ctile, ctile), ctile)
        power[at, :] = got[:, 0:128]
        gamps[at, :] = got[:, 128:256]
        gfilt[at, :] = got[:, 256:384]
        return 0

    lax.fori_loop(0, slots // ctile, conv_param, 0)

    measured[...] = jnp.zeros_like(measured)
    to_scalars.wait()

    own.wait()

    def wait_forward(k, _):
        forward(lax.rem(me + k, regions)).wait_send()
        return 0

    lax.fori_loop(1, regions, wait_forward, 0)

    def arrive_forward(k, _):
        frm = lax.rem(me + regions - k, regions)
        pltpu.make_async_remote_copy(
            src_ref=payload_ref.at[frm, 0:CAP],
            dst_ref=state.at[frm, 0:CAP],
            send_sem=fsend.at[frm],
            recv_sem=frecv.at[frm],
            device_id={"region": frm},
            device_id_type=MESH,
        ).wait_recv()
        return 0

    lax.fori_loop(1, regions, arrive_forward, 0)

    fault = (fnode_ref[...] - me * nodes).astype(F32)
    fault = jnp.concatenate([fault, fault], axis=1)
    conduct = 0.25 * jnp.left_shift(1, fkind_ref[...]).astype(F32)
    conduct = jnp.concatenate([conduct, conduct], axis=1)

    def line_copies(t):
        return [
            pltpu.make_async_remote_copy(
                src_ref=sendbuf.at[t, side],
                dst_ref=arrived.at[t, side],
                send_sem=lsend.at[t, side],
                recv_sem=lrecv.at[t, side],
                device_id={"region": to},
                device_id_type=MESH,
            )
            for side, to in ((0, nxt), (1, prv))
        ]

    def take_arrivals(t):
        for side, copy in enumerate(line_copies(t)):
            copy.wait()
            p = arrived[t, side]
            q = pltpu.roll(p, 64, 1)
            low = low_half(p.shape)
            hist[DMAX + t, side * LN : side * LN + 64, :] = jnp.where(low, p, q)
            hist[DMAX + t, side * LN + 64 : side * LN + 128, :] = jnp.where(low, q, p)

    def step(t, last):
        def conv(i, _):
            for q in range(pairs):
                for j in range(CAP):
                    measured[pl.ds(i * 128 + q * ROWS + j, 1), :] = volt[jnp.clip(index[i, q * ROWS + j], 0, nodes - 1)][None]
            at = pl.ds(pl.multiple_of(i * 128, 128), 128)
            m = measured[at, :]
            rows = pl.ds(i * pairs, pairs)
            f = state[rows].reshape(128, 128)
            low = low_half(f.shape)
            filt = f + gfilt[at, :] * (m - f)
            full = jnp.where(low, filt, pltpu.roll(filt, 64, 1))
            goal = power[at, :] * full / (1.0 + full * full)
            amps = f + gamps[at, :] * (goal - f)
            state[rows] = jnp.where(low, filt, amps).reshape(pairs, ROWS, 128)
            aop[at, :] = split(jnp.where(low, pltpu.roll(amps, 64, 1), amps))
            return 0

        lax.fori_loop(0, slots // 128, conv, 0)

        if last:

            backward(lax.rem(me + half, regions)).start()

            def start_backward(k, _):
                backward(lax.rem(me + half - k, regions)).start()
                backward(lax.rem(me + half + k, regions)).start()
                return 0

            lax.fori_loop(1, half, start_backward, 0)
            pltpu.make_async_copy(state.at[me, 0:CAP], ret.at[me, 0:CAP], bself).start()

        if t > 0:
            take_arrivals(t - 1)
        d = jnp.zeros((2 * LN, 128), F32)
        for k in range(1, DMAX + 1):
            d = d + jnp.where(ldelay[...] == float(k), hist[DMAX + t - k], 0.0)
        drive[...] = d
        aop[slots : slots + 2 * LN, :] = split(d)

        def assemble(i, _):
            at = pl.ds(pl.multiple_of(i * NTILE, NTILE), NTILE)
            z = both(jnp.dot(scat[at, :], aop[...], preferred_element_type=F32))
            v = volt[at, :]
            b = decay[at, :] * branch[at, :] + gain[at, :] * v
            branch[at, :] = b
            here = (lanes((NTILE, 128), 0) + i * NTILE).astype(F32)
            hit = jnp.where(fault == here, conduct * v, 0.0)
            x = split(source[at, :] - b - hit + z)
            for q in range(NTILE // BLK):
                xop[NTILE // BLK * i + q] = x[q * BLK : (q + 1) * BLK]
            return 0

        lax.fori_loop(0, nodes // NTILE, assemble, 0)

        def solve(i, _):
            found = []
            for q in range(GROUP):
                b = i * GROUP + q
                parts = [xop[cols_ref[k, b]] for k in range(KB)]
                x = jnp.concatenate(parts + [jnp.zeros((512 - KB * BLK, 128), BF16)], axis=0)
                z = jnp.dot(wmat[b], x, preferred_element_type=F32)
                found.append(both(z[0:BLK] + z[BLK : 2 * BLK]))
            at = pl.ds(pl.multiple_of(i * (GROUP * BLK), GROUP * BLK), GROUP * BLK)
            v = jnp.concatenate(found, axis=0)
            volt[at, :] = v
            env[at, :] = jnp.maximum(env[at, :], jnp.abs(v))
            return 0

        lax.fori_loop(0, NB // GROUP, solve, 0)

        def take_ends(i, _):
            for j in range(LN):
                ends[pl.ds(i * LN + j, 1), :] = volt[ends_ref[i, j]][None]
            return 0

        lax.fori_loop(0, 2, take_ends, 0)
        launch = ladm[...] * ends[...] - drive[...]
        low = low_half((64, 128))
        sendbuf[t, 0] = jnp.where(low, launch[LN : LN + 64], launch[LN + 64 : 2 * LN])
        sendbuf[t, 1] = jnp.where(low, launch[0:64], launch[64:LN])
        for copy in line_copies(t):
            copy.start()

    for t in range(STEPS):
        step(t, t == STEPS - 1)

    def peak(i, _):
        rows = []
        for q in range(8):
            at = pl.ds(pl.multiple_of((8 * i + q) * 128, 128), 128)
            rows.append(jnp.max(env[at, :].T, axis=0, keepdims=True))
        envbuf[sc, pl.ds(pl.multiple_of(8 * i, 8), 8), :] = jnp.concatenate(rows, axis=0)
        return 0

    lax.fori_loop(0, nodes // 1024, peak, 0)

    def env_copy(k):
        return pltpu.make_async_remote_copy(
            src_ref=envbuf.at[sc],
            dst_ref=envbuf.at[sc],
            send_sem=esend.at[k],
            recv_sem=erecv.at[k],
            device_id={"scen": lax.rem(sc + k, scens)},
            device_id_type=MESH,
        )

    for k in range(1, scens):
        env_copy(k).start()

    def finish(i, _):
        for q in range(4):
            at = pl.ds(pl.multiple_of((4 * i + q) * 128, 128), 128)
            volt_out[:, at] = volt[at, :].T[0:64]
            branch_out[:, at] = branch[at, :].T[0:64]
        return 0

    lax.fori_loop(0, nodes // 512, finish, 0)

    take_arrivals(STEPS - 1)
    for j in range(STEPS):
        for h in range(2):
            at = slice(h * 128, h * 128 + 128)
            wave_out[j, :, at] = hist[DMAX + STEPS - 1 - j, at, :].T[0:64]
    for j in range(STEPS, DMAX):
        wave_out[j] = winit_ref[j - STEPS]

    pltpu.make_async_copy(state.at[me, 0:CAP], ret.at[me, 0:CAP], bself).wait()

    def wait_backward(k, _):
        backward(lax.rem(me + k, regions)).wait_send()
        return 0

    lax.fori_loop(1, regions, wait_backward, 0)

    def arrive_backward(k, _):
        frm = lax.rem(me + regions - k, regions)
        pltpu.make_async_remote_copy(
            src_ref=state.at[frm, 0:CAP],
            dst_ref=ret.at[frm, 0:CAP],
            send_sem=bsend.at[frm],
            recv_sem=brecv.at[frm],
            device_id={"region": frm},
            device_id_type=MESH,
        ).wait_recv()
        return 0

    lax.fori_loop(1, regions, arrive_backward, 0)

    r = ret[...].reshape(slots, 128)
    lead = r.astype(BF16)
    rest = (r - lead.astype(F32)).astype(BF16)
    got = jnp.dot(back_ref[...], jnp.concatenate([lead, rest], axis=1), preferred_element_type=F32)
    got = got[:, 0:128] + got[:, 128:256]
    for c in range(got.shape[0] // 128):
        tile = got[c * 128 : c * 128 + 128].T
        conv_out[0, :, c * 128 : c * 128 + 128] = tile[0:64]
        conv_out[1, :, c * 128 : c * 128 + 128] = tile[64:128]

    for k in range(1, scens):
        env_copy(k).wait()
    best = envbuf[0]
    for k in range(1, scens):
        best = jnp.maximum(best, envbuf[k])
    env_out[...] = best


def deliver(*refs):
    count = len(refs[:-2]) // 3
    taken, given, held = refs[:count], refs[count : 2 * count], refs[2 * count : 3 * count]
    in_sem, out_sem = refs[-2:]
    ins = [pltpu.make_async_copy(taken[i], held[i], in_sem.at[i]) for i in range(count)]
    outs = [pltpu.make_async_copy(held[i], given[i], out_sem.at[i]) for i in range(count)]
    for copy in ins:
        copy.start()
    for copy, then in zip(ins, outs):
        copy.wait()
        then.start()
    for copy in outs:
        copy.wait()


def shards(
    regions,
    scens,
    inverse_blocks,
    block_cols,
    source_current,
    node_decay,
    node_gain,
    voltage_init,
    branch_init,
    wave_init,
    line_node,
    line_delay,
    line_admittance,
    conv_region,
    conv_node,
    conv_power,
    conv_gains,
    conv_init,
    fault_node,
    fault_kind,
):
    scen_count, nodes = voltage_init.shape
    convs = conv_node.shape[0]
    slots = regions * ROWS
    tiles = nodes // 128
    vm = pl.BlockSpec(memory_space=pltpu.VMEM)
    wide = pltpu.VMEM((nodes, 128), F32)
    dma = pltpu.SemaphoreType.DMA
    results = pl.pallas_call(
        functools.partial(kernel, regions, scens),
        out_shape=(
            jax.ShapeDtypeStruct(voltage_init.shape, F32),
            jax.ShapeDtypeStruct(voltage_init.shape, F32),
            jax.ShapeDtypeStruct(wave_init.shape, F32),
            jax.ShapeDtypeStruct(conv_init.shape, F32),
            jax.ShapeDtypeStruct((tiles, 128), F32),
        ),
        in_specs=[pl.BlockSpec(memory_space=pl.ANY)]
        + [pl.BlockSpec(memory_space=pltpu.SMEM)] * 2
        + [vm] * 16,
        out_specs=(vm,) * 5,
        scratch_shapes=[
            pltpu.VMEM((regions, ROWS, 128), F32),
            pltpu.VMEM((regions, 128), F32),
            pltpu.VMEM((convs, slots), BF16),
            pltpu.VMEM((NB, KB, BLK, BLK), F32),
            pltpu.VMEM((NB, 2 * BLK, 512), BF16),
            pltpu.VMEM((nodes, slots + 2 * LN), BF16),
            wide,
            wide,
            wide,
            wide,
            wide,
            wide,
            pltpu.VMEM((NB, BLK, 128), BF16),
            pltpu.VMEM((slots + 2 * LN, 128), BF16),
            pltpu.VMEM((slots, 128), F32),
            pltpu.VMEM((2 * LN, 128), F32),
            pltpu.VMEM((slots // 128, 128), jnp.int32),
            pltpu.SMEM((slots // 128, 128), jnp.int32),
            pltpu.VMEM((2 * LN, 128), F32),
            pltpu.VMEM((DMAX + STEPS, 2 * LN, 128), F32),
            pltpu.VMEM((regions, ROWS, 128), F32),
            pltpu.VMEM((regions, ROWS, 128), F32),
            pltpu.VMEM((slots, 128), F32),
            pltpu.VMEM((slots, 128), F32),
            pltpu.VMEM((slots, 128), F32),
            pltpu.VMEM((2 * LN, 128), F32),
            pltpu.VMEM((2 * LN, 128), F32),
            pltpu.VMEM((STEPS, 2, 64, 128), F32),
            pltpu.VMEM((STEPS, 2, 64, 128), F32),
            pltpu.VMEM((scens, tiles, 128), F32),
            dma,
            dma,
            dma((regions,)),
            dma((regions,)),
            dma,
            dma((regions,)),
            dma((regions,)),
            dma,
            dma((regions,)),
            dma((regions,)),
            dma,
            dma((STEPS, 2)),
            dma((STEPS, 2)),
            dma((scens,)),
            dma((scens,)),
        ],
        compiler_params=pltpu.CompilerParams(
            collective_id=0, has_side_effects=True, vmem_limit_bytes=67043328
        ),
        name="transient",
    )(
        inverse_blocks,
        block_cols.T,
        line_node.reshape(2, LN),
        voltage_init,
        branch_init,
        wave_init,
        conv_init,
        node_decay.reshape(tiles, 128),
        node_gain.reshape(tiles, 128),
        source_current.reshape(tiles, 128),
        line_node.reshape(2, LN),
        line_delay.reshape(2, LN),
        line_admittance.reshape(2, LN),
        conv_region.T,
        conv_node.reshape(convs // 128, 128),
        conv_power.reshape(convs // 128, 128),
        conv_gains,
        fault_node.reshape(1, scen_count),
        fault_kind.reshape(1, scen_count),
    )
    shapes = [jax.ShapeDtypeStruct(r.shape, r.dtype) for r in results]
    volt, branch, wave, conv, env = pl.pallas_call(
        deliver,
        out_shape=tuple(shapes),
        in_specs=[pl.BlockSpec(memory_space=pl.ANY)] * len(shapes),
        out_specs=(pl.BlockSpec(memory_space=pl.ANY),) * len(shapes),
        scratch_shapes=[pltpu.VMEM(r.shape, r.dtype) for r in shapes] + [dma((len(shapes),))] * 2,
        compiler_params=pltpu.CompilerParams(vmem_limit_bytes=67043328),
        name="deliver",
    )(*results)
    return (volt, branch, wave, conv, env.reshape(nodes))


def solution(mesh):
    placed = (
        P("region", None, None, None),
        P("region", None),
        P("region"),
        P("region"),
        P("region"),
        P("scen", "region"),
        P("scen", "region"),
        P(None, "scen", "region"),
        P("region"),
        P("region"),
        P("region"),
        P("region", None),
        P("region"),
        P("region"),
        P(None, "region"),
        P(None, "scen", "region"),
        P("scen"),
        P("scen"),
    )
    return jax.shard_map(
        functools.partial(shards, mesh.shape["region"], mesh.shape["scen"]),
        mesh=mesh,
        in_specs=placed,
        out_specs=(
            P("scen", "region"),
            P("scen", "region"),
            P(None, "scen", "region"),
            P(None, "scen", "region"),
            P("region"),
        ),
        check_vma=False,
    )
```

```python
import functools

import jax
import jax.numpy as jnp
from jax import lax
from jax.experimental import pallas as pl
from jax.experimental.pallas import tpu as pltpu
from jax.sharding import PartitionSpec as P

STEPS = 4
BLK = 96
KB = 5
NB = 32
CAP = 14
ROWS = 16
LN = 128
DMAX = 8
NTILE = 1536
GROUP = 16
MESH = pl.DeviceIdType.MESH
F32 = jnp.float32
BF16 = jnp.bfloat16


def lanes(shape, axis):
    return lax.broadcasted_iota(jnp.int32, shape, axis)


def low_half(shape):
    return lanes(shape, len(shape) - 1) % 128 < 64


def both(z):
    return z + pltpu.roll(z, 64, 1)


def split(x):
    lead = x.astype(BF16).astype(F32)
    return jnp.where(low_half(x.shape), lead, x - lead).astype(BF16)


def column(row):
    return jnp.broadcast_to(row, (128, 128)).T


def kernel(
    regions,
    scens,
    blocks_ref,
    cols_ref,
    ends_ref,
    vinit_ref,
    binit_ref,
    winit_ref,
    cinit_ref,
    decay_ref,
    gain_ref,
    source_ref,
    lnode_ref,
    ldelay_ref,
    ladm_ref,
    region_ref,
    cnode_ref,
    cpower_ref,
    cgains_ref,
    fnode_ref,
    fkind_ref,
    volt_out,
    branch_out,
    wave_out,
    conv_out,
    env_out,
    payload_ref,
    params_ref,
    back_ref,
    wraw,
    wmat,
    scat,
    volt,
    branch,
    env,
    decay,
    gain,
    source,
    xop,
    aop,
    measured,
    ends,
    indexv,
    index,
    drive,
    hist,
    state,
    ret,
    power,
    gamps,
    gfilt,
    ldelay,
    ladm,
    sendbuf,
    arrived,
    envbuf,
    load_sem,
    index_sem,
    psend,
    precv,
    pself,
    fsend,
    frecv,
    fself,
    bsend,
    brecv,
    bself,
    lsend,
    lrecv,
    esend,
    erecv,
):
    me = lax.axis_index("region")
    sc = lax.axis_index("scen")
    nxt = lax.rem(me + 1, regions)
    prv = lax.rem(me + regions - 1, regions)
    slots = regions * ROWS
    nodes = volt.shape[0]
    ctile = min(256, slots)
    pairs = 128 // ROWS

    state[:, CAP:, :] = jnp.zeros((regions, ROWS - CAP, 128), F32)
    ret[:, CAP:, :] = jnp.zeros((regions, ROWS - CAP, 128), F32)

    barrier = pltpu.get_barrier_semaphore()

    def greet(k, _):
        pl.semaphore_signal(
            barrier, inc=1, device_id={"region": lax.rem(me + k, regions)}, device_id_type=MESH
        )
        return 0

    lax.fori_loop(1, regions, greet, 0)
    for k in range(1, scens):
        pl.semaphore_signal(
            barrier, inc=1, device_id={"scen": lax.rem(sc + k, scens)}, device_id_type=MESH
        )
    load = pltpu.make_async_copy(blocks_ref, wraw, load_sem)
    load.start()

    convs = back_ref.shape[0]
    lane = lanes((convs, 128), 1)
    target = jnp.concatenate(
        [column(region_ref[:, h * 128 : h * 128 + 128].astype(F32)) for h in range(convs // 128)], axis=0
    )
    member = jnp.where(target == lane.astype(F32), 1.0, 0.0)
    before = jnp.where(lanes((convs, convs), 0) > lanes((convs, convs), 1), 1.0, 0.0)
    earlier = jnp.dot(before.astype(BF16), member.astype(BF16), preferred_element_type=F32)
    rank = jnp.sum(earlier * member, axis=1, keepdims=True)
    position = target * float(ROWS) + rank
    for c in range(slots // 128):
        back_ref[:, c * 128 : c * 128 + 128] = jnp.where(
            position == (lane + c * 128).astype(F32), 1.0, 0.0
        ).astype(BF16)
    content = jnp.concatenate([cinit_ref[0], cinit_ref[1]], axis=0)
    lead = content.astype(BF16)
    rest = (content - lead.astype(F32)).astype(BF16)
    content = jnp.dot(
        jnp.concatenate([lead, rest], axis=0), back_ref[...], preferred_element_type=F32
    )
    content = content[0:128] + content[128:256]
    for c in range(slots // 128):
        payload_ref[c * pairs : c * pairs + pairs] = content[:, c * 128 : c * 128 + 128].T.reshape(
            pairs, ROWS, 128
        )
    params = jnp.concatenate(
        [
            jnp.concatenate(
                [
                    cnode_ref[h : h + 1, :].astype(F32) + 1.0,
                    cpower_ref[h : h + 1, :],
                    cgains_ref[:, h * 128 : h * 128 + 128],
                    jnp.zeros((124, 128), F32),
                ],
                axis=0,
            ).T
            for h in range(convs // 128)
        ],
        axis=0,
    )
    values = jnp.zeros((convs, 128), F32)
    for w in range(4):
        values = values + jnp.where(lane // ROWS == w, params[:, w : w + 1], 0.0)
    values = jnp.where((lane % ROWS).astype(F32) == rank, values, 0.0)
    lead = values.astype(BF16).astype(F32)
    values = jnp.where(lane < 64, lead, pltpu.roll(values - lead, 64, 1)).astype(BF16)
    owners = jnp.concatenate(
        [member[h * 128 : h * 128 + 128].T for h in range(convs // 128)], axis=1
    ).astype(BF16)
    payload_ref[:, CAP, :] = both(jnp.dot(owners, values, preferred_element_type=F32))[0:regions]

    pl.semaphore_wait(barrier, regions - 1 + scens - 1)

    def forward(peer):
        return pltpu.make_async_remote_copy(
            src_ref=payload_ref.at[peer, 0:CAP],
            dst_ref=state.at[me, 0:CAP],
            send_sem=fsend.at[peer],
            recv_sem=frecv.at[me],
            device_id={"region": peer},
            device_id_type=MESH,
        )

    def announce(peer):
        return pltpu.make_async_remote_copy(
            src_ref=payload_ref.at[peer, CAP],
            dst_ref=params_ref.at[me],
            send_sem=psend.at[peer],
            recv_sem=precv.at[me],
            device_id={"region": peer},
            device_id_type=MESH,
        )

    def backward(peer):
        return pltpu.make_async_remote_copy(
            src_ref=state.at[peer, 0:CAP],
            dst_ref=ret.at[me, 0:CAP],
            send_sem=bsend.at[peer],
            recv_sem=brecv.at[me],
            device_id={"region": peer},
            device_id_type=MESH,
        )

    half = regions // 2
    announce(lax.rem(me + half, regions)).start()

    def start_announce(k, _):
        announce(lax.rem(me + half - k, regions)).start()
        announce(lax.rem(me + half + k, regions)).start()
        return 0

    lax.fori_loop(1, half, start_announce, 0)
    own_params = pltpu.make_async_copy(payload_ref.at[me, CAP], params_ref.at[me], pself)
    own_params.start()
    forward(lax.rem(me + half, regions)).start()

    def start_forward(k, _):
        forward(lax.rem(me + half - k, regions)).start()
        forward(lax.rem(me + half + k, regions)).start()
        return 0

    lax.fori_loop(1, half, start_forward, 0)
    own = pltpu.make_async_copy(payload_ref.at[me, 0:CAP], state.at[me, 0:CAP], fself)
    own.start()

    def place(i, _):
        for q in range(2):
            c = 2 * i + q
            at = pl.ds(pl.multiple_of(c * 128, 128), 128)
            v = vinit_ref[:, at]
            volt[at, :] = jnp.concatenate([v, v], axis=0).T
            b = binit_ref[:, at]
            branch[at, :] = jnp.concatenate([b, b], axis=0).T
            decay[at, :] = column(decay_ref[pl.ds(c, 1), :])
            gain[at, :] = column(gain_ref[pl.ds(c, 1), :])
            source[at, :] = column(source_ref[pl.ds(c, 1), :])
            env[at, :] = jnp.zeros((128, 128), F32)
        return 0

    lax.fori_loop(0, nodes // 256, place, 0)

    def place_wave(d, _):
        for h in range(2):
            w = winit_ref[d, :, h * 128 : h * 128 + 128]
            hist[DMAX - 1 - d, h * 128 : h * 128 + 128, :] = jnp.concatenate([w, w], axis=0).T
        return 0

    lax.fori_loop(0, DMAX, place_wave, 0)

    for h in range(2):
        at = slice(h * 128, h * 128 + 128)
        ldelay[at, :] = column(ldelay_ref[h : h + 1, :].astype(F32))
        ladm[at, :] = 2.0 * column(ladm_ref[h : h + 1, :])
        def line_scatter(c, _):
            here = (lanes((128, 128), 0) + c * 128).astype(F32)
            row = lnode_ref[h : h + 1, :].astype(F32)
            scat[pl.ds(pl.multiple_of(c * 128, 128), 128), slots + h * 128 : slots + h * 128 + 128] = (
                jnp.where(row == here, 1.0, 0.0).astype(BF16)
            )
            return 0

        lax.fori_loop(0, nodes // 128, line_scatter, 0)

    load.wait()

    def prepare(b, _):
        parts = [wraw[b, k] for k in range(KB)]
        whole = jnp.concatenate(parts + [jnp.zeros((BLK, 512 - KB * BLK), F32)], axis=1)
        lead = whole.astype(BF16)
        wmat[b, 0:BLK, :] = lead
        wmat[b, BLK : 2 * BLK, :] = (whole - lead.astype(F32)).astype(BF16)
        return 0

    lax.fori_loop(0, NB, prepare, 0)

    own_params.wait()

    def wait_announce(k, _):
        announce(lax.rem(me + k, regions)).wait_send()
        return 0

    lax.fori_loop(1, regions, wait_announce, 0)

    def arrive_announce(k, _):
        frm = lax.rem(me + regions - k, regions)
        pltpu.make_async_remote_copy(
            src_ref=payload_ref.at[frm, CAP],
            dst_ref=params_ref.at[frm],
            send_sem=psend.at[frm],
            recv_sem=precv.at[frm],
            device_id={"region": frm},
            device_id_type=MESH,
        ).wait_recv()
        return 0

    lax.fori_loop(1, regions, arrive_announce, 0)

    params = params_ref[...]
    lead = params.astype(BF16).astype(F32)
    lane64 = lanes((regions, 128), 1) < 64
    pair = jnp.where(lane64, lead, pltpu.roll(params - lead, 64, 1))
    fold = (lanes((128, slots), 0) % 64 == lanes((128, slots), 1) % ROWS).astype(F32).astype(BF16)
    spread = jnp.dot(pair.astype(BF16), fold, preferred_element_type=F32)
    mine = lanes((regions, slots), 0) == lanes((regions, slots), 1) // ROWS
    noderow = jnp.sum(jnp.where(mine, spread, 0.0), axis=0, keepdims=True)

    for r in range(slots // 128):
        number = noderow[:, r * 128 : r * 128 + 128].astype(jnp.int32) - 1
        indexv[r : r + 1, :] = jnp.clip(number, 0, nodes - 1)
    to_scalars = pltpu.make_async_copy(indexv, index, index_sem)
    to_scalars.start()

    def conv_scatter(c, _):
        here = (lanes((128, slots), 0) + (c * 128 + 1)).astype(F32)
        scat[pl.ds(pl.multiple_of(c * 128, 128), 128), 0:slots] = (
            jnp.where(noderow == here, 1.0, 0.0).astype(BF16)
        )
        return 0

    lax.fori_loop(0, nodes // 128, conv_scatter, 0)

    pick = ((lanes((128, 384), 0) % 64) // ROWS == lanes((128, 384), 1) // 128 + 1).astype(F32).astype(BF16)

    def conv_param(i, _):
        r0 = i * (ctile // ROWS)
        prm = params_ref[pl.ds(r0, ctile // ROWS), :]
        ld = prm.astype(BF16).astype(F32)
        both_parts = jnp.where(low_half(prm.shape), ld, pltpu.roll(prm - ld, 64, 1))
        rep = jnp.broadcast_to(both_parts[:, None, :], (ctile // ROWS, ROWS, 128)).reshape(ctile, 128)
        slot = lanes((ctile, 128), 0) % ROWS
        rep = jnp.where(lanes((ctile, 128), 1) % ROWS == slot, rep, 0.0).astype(BF16)
        got = jnp.dot(rep, pick, preferred_element_type=F32)
        at = pl.ds(pl.multiple_of(i * ctile, ctile), ctile)
        power[at, :] = got[:, 0:128]
        gamps[at, :] = got[:, 128:256]
        gfilt[at, :] = got[:, 256:384]
        return 0

    lax.fori_loop(0, slots // ctile, conv_param, 0)

    measured[...] = jnp.zeros_like(measured)
    to_scalars.wait()

    own.wait()

    def wait_forward(k, _):
        forward(lax.rem(me + k, regions)).wait_send()
        return 0

    lax.fori_loop(1, regions, wait_forward, 0)

    def arrive_forward(k, _):
        frm = lax.rem(me + regions - k, regions)
        pltpu.make_async_remote_copy(
            src_ref=payload_ref.at[frm, 0:CAP],
            dst_ref=state.at[frm, 0:CAP],
            send_sem=fsend.at[frm],
            recv_sem=frecv.at[frm],
            device_id={"region": frm},
            device_id_type=MESH,
        ).wait_recv()
        return 0

    lax.fori_loop(1, regions, arrive_forward, 0)

    fault = (fnode_ref[...] - me * nodes).astype(F32)
    fault = jnp.concatenate([fault, fault], axis=1)
    conduct = 0.25 * jnp.left_shift(1, fkind_ref[...]).astype(F32)
    conduct = jnp.concatenate([conduct, conduct], axis=1)

    def line_copies(t):
        return [
            pltpu.make_async_remote_copy(
                src_ref=sendbuf.at[t, side],
                dst_ref=arrived.at[t, side],
                send_sem=lsend.at[t, side],
                recv_sem=lrecv.at[t, side],
                device_id={"region": to},
                device_id_type=MESH,
            )
            for side, to in ((0, nxt), (1, prv))
        ]

    def take_arrivals(t):
        for side, copy in enumerate(line_copies(t)):
            copy.wait()
            p = arrived[t, side]
            q = pltpu.roll(p, 64, 1)
            low = low_half(p.shape)
            hist[DMAX + t, side * LN : side * LN + 64, :] = jnp.where(low, p, q)
            hist[DMAX + t, side * LN + 64 : side * LN + 128, :] = jnp.where(low, q, p)

    def step(t, last):
        def conv(i, _):
            for q in range(2 * pairs):
                for j in range(CAP):
                    number = index[2 * i + q // pairs, q % pairs * ROWS + j]
                    measured[pl.ds(i * 256 + q * ROWS + j, 1), :] = volt[jnp.clip(number, 0, nodes - 1)][None]
            at = pl.ds(pl.multiple_of(i * 256, 256), 256)
            m = measured[at, :]
            rows = pl.ds(i * 2 * pairs, 2 * pairs)
            f = state[rows].reshape(256, 128)
            low = low_half(f.shape)
            filt = f + gfilt[at, :] * (m - f)
            full = jnp.where(low, filt, pltpu.roll(filt, 64, 1))
            goal = power[at, :] * full / (1.0 + full * full)
            amps = f + gamps[at, :] * (goal - f)
            state[rows] = jnp.where(low, filt, amps).reshape(2 * pairs, ROWS, 128)
            aop[at, :] = split(jnp.where(low, pltpu.roll(amps, 64, 1), amps))
            return 0

        lax.fori_loop(0, slots // 256, conv, 0)

        if last:

            backward(lax.rem(me + half, regions)).start()

            def start_backward(k, _):
                backward(lax.rem(me + half - k, regions)).start()
                backward(lax.rem(me + half + k, regions)).start()
                return 0

            lax.fori_loop(1, half, start_backward, 0)
            pltpu.make_async_copy(state.at[me, 0:CAP], ret.at[me, 0:CAP], bself).start()

        if t > 0:
            take_arrivals(t - 1)
        d = jnp.zeros((2 * LN, 128), F32)
        for k in range(1, DMAX + 1):
            d = d + jnp.where(ldelay[...] == float(k), hist[DMAX + t - k], 0.0)
        drive[...] = d
        aop[slots : slots + 2 * LN, :] = split(d)

        def assemble(i, _):
            at = pl.ds(pl.multiple_of(i * NTILE, NTILE), NTILE)
            z = both(jnp.dot(scat[at, :], aop[...], preferred_element_type=F32))
            v = volt[at, :]
            b = decay[at, :] * branch[at, :] + gain[at, :] * v
            branch[at, :] = b
            here = (lanes((NTILE, 128), 0) + i * NTILE).astype(F32)
            hit = jnp.where(fault == here, conduct * v, 0.0)
            x = split(source[at, :] - b - hit + z)
            for q in range(NTILE // BLK):
                xop[NTILE // BLK * i + q] = x[q * BLK : (q + 1) * BLK]
            return 0

        lax.fori_loop(0, nodes // NTILE, assemble, 0)

        def solve(i, _):
            found = []
            for q in range(GROUP):
                b = i * GROUP + q
                parts = [xop[cols_ref[k, b]] for k in range(KB)]
                x = jnp.concatenate(parts + [jnp.zeros((512 - KB * BLK, 128), BF16)], axis=0)
                z = jnp.dot(wmat[b], x, preferred_element_type=F32)
                found.append(both(z[0:BLK] + z[BLK : 2 * BLK]))
            at = pl.ds(pl.multiple_of(i * (GROUP * BLK), GROUP * BLK), GROUP * BLK)
            v = jnp.concatenate(found, axis=0)
            volt[at, :] = v
            env[at, :] = jnp.maximum(env[at, :], jnp.abs(v))
            return 0

        lax.fori_loop(0, NB // GROUP, solve, 0)

        def take_ends(i, _):
            for j in range(LN):
                ends[pl.ds(i * LN + j, 1), :] = volt[ends_ref[i, j]][None]
            return 0

        lax.fori_loop(0, 2, take_ends, 0)
        launch = ladm[...] * ends[...] - drive[...]
        low = low_half((64, 128))
        sendbuf[t, 0] = jnp.where(low, launch[LN : LN + 64], launch[LN + 64 : 2 * LN])
        sendbuf[t, 1] = jnp.where(low, launch[0:64], launch[64:LN])
        for copy in line_copies(t):
            copy.start()

    for t in range(STEPS):
        step(t, t == STEPS - 1)

    def peak(i, _):
        rows = []
        for q in range(8):
            at = pl.ds(pl.multiple_of((8 * i + q) * 128, 128), 128)
            rows.append(jnp.max(env[at, :].T, axis=0, keepdims=True))
        envbuf[sc, pl.ds(pl.multiple_of(8 * i, 8), 8), :] = jnp.concatenate(rows, axis=0)
        return 0

    lax.fori_loop(0, nodes // 1024, peak, 0)

    def env_copy(k):
        return pltpu.make_async_remote_copy(
            src_ref=envbuf.at[sc],
            dst_ref=envbuf.at[sc],
            send_sem=esend.at[k],
            recv_sem=erecv.at[k],
            device_id={"scen": lax.rem(sc + k, scens)},
            device_id_type=MESH,
        )

    for k in range(1, scens):
        env_copy(k).start()

    def finish(i, _):
        for q in range(4):
            at = pl.ds(pl.multiple_of((4 * i + q) * 128, 128), 128)
            volt_out[:, at] = volt[at, :].T[0:64]
            branch_out[:, at] = branch[at, :].T[0:64]
        return 0

    lax.fori_loop(0, nodes // 512, finish, 0)

    take_arrivals(STEPS - 1)
    for j in range(STEPS):
        for h in range(2):
            at = slice(h * 128, h * 128 + 128)
            wave_out[j, :, at] = hist[DMAX + STEPS - 1 - j, at, :].T[0:64]
    for j in range(STEPS, DMAX):
        wave_out[j] = winit_ref[j - STEPS]

    pltpu.make_async_copy(state.at[me, 0:CAP], ret.at[me, 0:CAP], bself).wait()

    def wait_backward(k, _):
        backward(lax.rem(me + k, regions)).wait_send()
        return 0

    lax.fori_loop(1, regions, wait_backward, 0)

    def arrive_backward(k, _):
        frm = lax.rem(me + regions - k, regions)
        pltpu.make_async_remote_copy(
            src_ref=state.at[frm, 0:CAP],
            dst_ref=ret.at[frm, 0:CAP],
            send_sem=bsend.at[frm],
            recv_sem=brecv.at[frm],
            device_id={"region": frm},
            device_id_type=MESH,
        ).wait_recv()
        return 0

    lax.fori_loop(1, regions, arrive_backward, 0)

    r = ret[...].reshape(slots, 128)
    lead = r.astype(BF16)
    rest = (r - lead.astype(F32)).astype(BF16)
    got = jnp.dot(back_ref[...], jnp.concatenate([lead, rest], axis=1), preferred_element_type=F32)
    got = got[:, 0:128] + got[:, 128:256]
    for c in range(got.shape[0] // 128):
        tile = got[c * 128 : c * 128 + 128].T
        conv_out[0, :, c * 128 : c * 128 + 128] = tile[0:64]
        conv_out[1, :, c * 128 : c * 128 + 128] = tile[64:128]

    for k in range(1, scens):
        env_copy(k).wait()
    best = envbuf[0]
    for k in range(1, scens):
        best = jnp.maximum(best, envbuf[k])
    env_out[...] = best


def deliver(*refs):
    count = len(refs[:-2]) // 3
    taken, given, held = refs[:count], refs[count : 2 * count], refs[2 * count : 3 * count]
    in_sem, out_sem = refs[-2:]
    ins = [pltpu.make_async_copy(taken[i], held[i], in_sem.at[i]) for i in range(count)]
    outs = [pltpu.make_async_copy(held[i], given[i], out_sem.at[i]) for i in range(count)]
    for copy in ins:
        copy.start()
    for copy, then in zip(ins, outs):
        copy.wait()
        then.start()
    for copy in outs:
        copy.wait()


def shards(
    regions,
    scens,
    inverse_blocks,
    block_cols,
    source_current,
    node_decay,
    node_gain,
    voltage_init,
    branch_init,
    wave_init,
    line_node,
    line_delay,
    line_admittance,
    conv_region,
    conv_node,
    conv_power,
    conv_gains,
    conv_init,
    fault_node,
    fault_kind,
):
    scen_count, nodes = voltage_init.shape
    convs = conv_node.shape[0]
    slots = regions * ROWS
    tiles = nodes // 128
    vm = pl.BlockSpec(memory_space=pltpu.VMEM)
    wide = pltpu.VMEM((nodes, 128), F32)
    dma = pltpu.SemaphoreType.DMA
    results = pl.pallas_call(
        functools.partial(kernel, regions, scens),
        out_shape=(
            jax.ShapeDtypeStruct(voltage_init.shape, F32),
            jax.ShapeDtypeStruct(voltage_init.shape, F32),
            jax.ShapeDtypeStruct(wave_init.shape, F32),
            jax.ShapeDtypeStruct(conv_init.shape, F32),
            jax.ShapeDtypeStruct((tiles, 128), F32),
        ),
        in_specs=[pl.BlockSpec(memory_space=pl.ANY)]
        + [pl.BlockSpec(memory_space=pltpu.SMEM)] * 2
        + [vm] * 16,
        out_specs=(vm,) * 5,
        scratch_shapes=[
            pltpu.VMEM((regions, ROWS, 128), F32),
            pltpu.VMEM((regions, 128), F32),
            pltpu.VMEM((convs, slots), BF16),
            pltpu.VMEM((NB, KB, BLK, BLK), F32),
            pltpu.VMEM((NB, 2 * BLK, 512), BF16),
            pltpu.VMEM((nodes, slots + 2 * LN), BF16),
            wide,
            wide,
            wide,
            wide,
            wide,
            wide,
            pltpu.VMEM((NB, BLK, 128), BF16),
            pltpu.VMEM((slots + 2 * LN, 128), BF16),
            pltpu.VMEM((slots, 128), F32),
            pltpu.VMEM((2 * LN, 128), F32),
            pltpu.VMEM((slots // 128, 128), jnp.int32),
            pltpu.SMEM((slots // 128, 128), jnp.int32),
            pltpu.VMEM((2 * LN, 128), F32),
            pltpu.VMEM((DMAX + STEPS, 2 * LN, 128), F32),
            pltpu.VMEM((regions, ROWS, 128), F32),
            pltpu.VMEM((regions, ROWS, 128), F32),
            pltpu.VMEM((slots, 128), F32),
            pltpu.VMEM((slots, 128), F32),
            pltpu.VMEM((slots, 128), F32),
            pltpu.VMEM((2 * LN, 128), F32),
            pltpu.VMEM((2 * LN, 128), F32),
            pltpu.VMEM((STEPS, 2, 64, 128), F32),
            pltpu.VMEM((STEPS, 2, 64, 128), F32),
            pltpu.VMEM((scens, tiles, 128), F32),
            dma,
            dma,
            dma((regions,)),
            dma((regions,)),
            dma,
            dma((regions,)),
            dma((regions,)),
            dma,
            dma((regions,)),
            dma((regions,)),
            dma,
            dma((STEPS, 2)),
            dma((STEPS, 2)),
            dma((scens,)),
            dma((scens,)),
        ],
        compiler_params=pltpu.CompilerParams(
            collective_id=0, has_side_effects=True, vmem_limit_bytes=67043328
        ),
        name="transient",
    )(
        inverse_blocks,
        block_cols.T,
        line_node.reshape(2, LN),
        voltage_init,
        branch_init,
        wave_init,
        conv_init,
        node_decay.reshape(tiles, 128),
        node_gain.reshape(tiles, 128),
        source_current.reshape(tiles, 128),
        line_node.reshape(2, LN),
        line_delay.reshape(2, LN),
        line_admittance.reshape(2, LN),
        conv_region.T,
        conv_node.reshape(convs // 128, 128),
        conv_power.reshape(convs // 128, 128),
        conv_gains,
        fault_node.reshape(1, scen_count),
        fault_kind.reshape(1, scen_count),
    )
    shapes = [jax.ShapeDtypeStruct(r.shape, r.dtype) for r in results]
    volt, branch, wave, conv, env = pl.pallas_call(
        deliver,
        out_shape=tuple(shapes),
        in_specs=[pl.BlockSpec(memory_space=pl.ANY)] * len(shapes),
        out_specs=(pl.BlockSpec(memory_space=pl.ANY),) * len(shapes),
        scratch_shapes=[pltpu.VMEM(r.shape, r.dtype) for r in shapes] + [dma((len(shapes),))] * 2,
        compiler_params=pltpu.CompilerParams(vmem_limit_bytes=67043328),
        name="deliver",
    )(*results)
    return (volt, branch, wave, conv, env.reshape(nodes))


def solution(mesh):
    placed = (
        P("region", None, None, None),
        P("region", None),
        P("region"),
        P("region"),
        P("region"),
        P("scen", "region"),
        P("scen", "region"),
        P(None, "scen", "region"),
        P("region"),
        P("region"),
        P("region"),
        P("region", None),
        P("region"),
        P("region"),
        P(None, "region"),
        P(None, "scen", "region"),
        P("scen"),
        P("scen"),
    )
    return jax.shard_map(
        functools.partial(shards, mesh.shape["region"], mesh.shape["scen"]),
        mesh=mesh,
        in_specs=placed,
        out_specs=(
            P("scen", "region"),
            P("scen", "region"),
            P(None, "scen", "region"),
            P(None, "scen", "region"),
            P("region"),
        ),
        check_vma=False,
    )
```
